128 devices in a mesh: scen: 8 (over z_lo, x), opt: 16 (over z_hi, y, core).
Axes of the slice: x: 4, y: 4, z: 4 (z_hi: 2, z_lo: 2; z = z_hi * 2 + z_lo), core: 2. Of those that a mesh axis runs over, the one named last changes fastest.
Arguments:
- option_coefs: float32 [16384, 1024], P(('opt', 'scen')), may hold values from -0.75 to 0.75
- underlying_of: int32 [16384, 1], P('opt'), may hold values from 0 to 127; in each aligned block of 128 rows (0 to 127, 128 to 255, ...) at most 2 rows name the same one
- log_return_mean: float32 [128, 2048], P(('scen', 'opt')), may hold values from -1 to 1
- log_return_spread: float32 [128, 2048], P(('scen', 'opt')), may hold values from 1e-06 to 0.0001
- cost: float32 [16384], P('opt'), may hold values from -3 to 3
- positions: float32 [16384], P('opt'), may hold values from -1 to 1
- base_loss: float32 [2048], P('scen'), may hold values from -6 to 6
- duals: float32 [2048], P('scen'), may hold values from 0 to 1
- threshold: float32 [1], replicated, may hold values from -2 to 2
Outputs:
- scenario_values: float32 [16384, 2048], P('opt', 'scen')
- new_positions: float32 [16384], P('opt')
- new_duals: float32 [2048], P('scen')
- new_threshold: float32 [1], replicated
The draws below stay inside these ranges and needn't reach their ends.
Inputs may be any that keep to these rules, and one draw needn't show every extreme that they name: `underlying_of`: in each aligned block of 128 options no underlying is named more than 2 times, a bound that some block reaches; every underlying is named somewhere.
All inputs are finite; a program needn't handle non-finite values.
Results may differ from the reference program's by a relative error of at most 0.0003.
Values sent between devices are 32-bit elements; how exact they have to be, the bound alone decides.
No kernel may reach another device: no remote copies, remote signals or barrier semaphores. Data moves between devices by JAX's collectives and lax.ppermute only.
A program may use at most 64 MiB of HBM per device.

```python
import math
import jax
import jax.numpy as jnp
import numpy as np
from jax import lax

TERMS = 1024
OPT_DEV = 128
ITERS = 2
SCENARIOS = 2048
OPTIONS = 16384
UNDERLYINGS = 128
MOST = 2


def draw_duals(key, part):
    position = jnp.arange(SCENARIOS, dtype=jnp.float32) / SCENARIOS
    rising = 0.25 + 0.75 * position
    uniform_draw = jax.random.uniform(key, (SCENARIOS,), jnp.float32, 0.0, 1.0)
    return jnp.clip(rising * uniform_draw, 0.0, 1.0)


def level_of(rng, dims, cuts, smallest, high):
    level = 1.0
    for axis_at, parts in cuts:
        draws = jax.random.uniform(jax.random.fold_in(jax.random.fold_in(rng, 6), axis_at), (parts,), jnp.float32, smallest / len(cuts), high / len(cuts))
        level = level * jnp.repeat(jnp.exp(draws), dims[axis_at] // parts).reshape((-1,) + (1,) * (len(dims) - 1 - axis_at))
    return level


def shared_out(key, own, number, rows, amount, top, limit, slope):
    ranking = jax.random.permutation(key, amount)
    heavy_load, usual = shares(amount, rows * top, limit, slope, True), shares(amount, rows * top, limit, slope, False)
    places = jnp.arange(amount)

    def named(sizes, offset_by):
        used = int((sizes > 0).sum())
        fixed = max(1, used // 4)
        shifted = fixed + (places - fixed + offset_by * (used - fixed)) % max(1, amount - fixed)
        return jnp.zeros((amount,), jnp.int32).at[ranking[jnp.where(places < fixed, places, shifted)]].set(jnp.asarray(sizes, jnp.int32))

    sizes = jnp.where(number % 4 == 0, named(heavy_load, number // 4), named(usual, number - number // 4 - 1))
    mixed = jax.random.permutation(jax.random.fold_in(own, 3), amount)
    source_of, taker = mixed[0:amount // 2 * 2:2], mixed[1:amount // 2 * 2:2]
    slack = jnp.minimum(sizes[source_of] - 1, limit - sizes[taker]) // 2
    slack = jnp.where((source_of == ranking[0]) | (taker == ranking[0]) | (sizes[taker] == 0), 0, jnp.maximum(slack, 0))
    shifted = jax.random.randint(jax.random.fold_in(own, 4), (amount // 2,), 0, 1 << 20) % (slack + 1)
    sizes = sizes.at[source_of].add(-shifted).at[taker].add(shifted)
    items = jnp.searchsorted(jnp.cumsum(sizes), jnp.arange(rows * top), side="right").astype(jnp.int32)
    table = items.reshape(top, rows).T
    table = table[jax.random.permutation(jax.random.fold_in(own, 1), rows)]
    offset_by = jax.random.randint(jax.random.fold_in(own, 2), (rows, 1), 0, top)
    return jnp.take_along_axis(table, (jnp.arange(top)[None, :] + offset_by) % top, axis=1)


def shares(amount, total, limit, skew, full):
    weights = [(1 << 20) // math.isqrt(rank ** skew) + 1 for rank in range(1, amount + 1)]
    largest = limit if full else min(limit, max(-(-total // amount), total * weights[0] // sum(weights)))
    least = 1 if total - largest >= amount - 1 else 0
    given, surplus = [largest] + [least] * (amount - 1), total - largest - least * (amount - 1)
    while surplus > 0:
        movable = [i for i in range(1, amount) if given[i] < largest] or [i for i in range(1, amount) if given[i] < limit]
        mass, budget = sum([weights[i] for i in movable]), surplus
        for i in movable:
            addition = min(limit - given[i], max(1, budget * weights[i] // mass), surplus)
            given[i] = given[i] + addition
            surplus = surplus - addition
    return np.array(given)


def centred(key, extent, scale, bound, split=(), kind=jnp.bfloat16):
    gain = level_of(key, extent, split, -0.22, 0.18) if split else 1.0
    drawn = jax.random.normal(key, extent, jnp.float32) * scale * gain
    return jnp.minimum(jnp.maximum(drawn, -bound), bound).astype(kind)


def setup_inputs(seed: int = 0) -> dict:
    keys = jax.random.split(jax.random.key(seed), 10)
    option_coefs = centred(keys[0], (OPTIONS, TERMS), 0.125, 0.75, ((0, 128),), jnp.float32)
    underlying_of_keys = jax.random.split(jax.random.fold_in(keys[1], 1), OPTIONS // OPT_DEV)
    underlying_of_turns = jax.random.permutation(jax.random.fold_in(keys[1], 3), OPTIONS // OPT_DEV)
    underlying_of = jax.vmap(lambda own, number: shared_out(jax.random.fold_in(keys[1], 2), own, number, OPT_DEV, UNDERLYINGS, 1, MOST, 2))(underlying_of_keys, underlying_of_turns).reshape((OPTIONS, 1))
    log_return_mean = jnp.clip(jax.random.uniform(keys[2], (UNDERLYINGS, SCENARIOS), jnp.float32, -1.0, 1.0) * level_of(keys[2], (UNDERLYINGS, SCENARIOS), ((0, 128),), -0.4, 0.0), -1.0, 1.0)
    log_return_spread = jnp.clip(jnp.exp(math.log(0.0001) - 4.6051702 * jax.random.uniform(keys[3], (UNDERLYINGS, SCENARIOS), jnp.float32) ** level_of(keys[3], (UNDERLYINGS, SCENARIOS), ((0, 128),), -0.2, 0.2)), 9.999999974752427e-07, 0.0001)
    cost = centred(keys[4], (OPTIONS,), 0.5, 3.0, ((0, 16),), jnp.float32)
    positions = jnp.clip(jax.random.uniform(keys[5], (OPTIONS,), jnp.float32, -1.0, 1.0) * level_of(keys[5], (OPTIONS,), ((0, 16),), -0.4, 0.0), -1.0, 1.0)
    base_loss = centred(keys[6], (SCENARIOS,), 1.0, 6.0, ((0, 8),), jnp.float32)
    duals = draw_duals(jax.random.fold_in(keys[9], 71), 0)
    threshold = centred(keys[8], (1,), 0.5, 2.0, (), jnp.float32)
    return dict(option_coefs=option_coefs, underlying_of=underlying_of, log_return_mean=log_return_mean, log_return_spread=log_return_spread, cost=cost, positions=positions, base_loss=base_loss, duals=duals, threshold=threshold)


LOW_END = -4.0
HIGH_END = 4.0
TAIL_LEVEL = 0.9
PRIMAL_STEP = 0.5
THRESH_STEP = 0.05
DUAL_STEP = 0.5

def cosine_terms(drift_rows, variance_rows, term_count):
    frequency = jnp.arange(term_count, dtype=jnp.float32) * (math.pi / (HIGH_END - LOW_END))
    weight = jnp.where(jnp.arange(term_count) == 0, 0.5, 1.0).astype(jnp.float32) * (2.0 / (HIGH_END - LOW_END))
    decay = jnp.exp(-0.5 * variance_rows[:, None] * frequency * frequency)
    return weight * decay * jnp.cos(frequency * (drift_rows[:, None] - LOW_END))

def reference(option_coefs, underlying_of, log_return_mean, log_return_spread, cost, positions, base_loss, duals, threshold):
    owners = underlying_of[:, 0].reshape(-1, OPT_DEV)
    blocks = owners.shape[0]
    onehot = (owners[..., None] == jnp.arange(UNDERLYINGS, dtype=jnp.int32)).astype(jnp.int32)
    slot_rank = lax.optimization_barrier(jnp.sum((jnp.cumsum(onehot, axis=1) - onehot) * onehot, axis=-1))
    place_offset_number = (jnp.arange(blocks, dtype=jnp.int32)[:, None] * MOST + slot_rank).reshape(-1).astype(jnp.int32)
    linear_holder_number = owners.reshape(-1).astype(jnp.int32)
    resorted_worths = jnp.zeros((UNDERLYINGS, blocks * MOST, TERMS), jnp.float32).at[linear_holder_number, place_offset_number].set(option_coefs)

    def contract_cost_holder(operands):
        drift_rows, variance_rows, coef_rows = operands
        cosine_table = cosine_terms(drift_rows, variance_rows, TERMS)
        return jnp.dot(coef_rows, cosine_table.T, precision=lax.Precision.HIGHEST)
    valued_contracts = lax.map(contract_cost_holder, (log_return_mean, log_return_spread, resorted_worths))
    contract_worths = valued_contracts[linear_holder_number, place_offset_number]
    holding = positions
    weights = duals
    level = threshold[0]
    for iteration in range(ITERS):
        gradient = cost - jnp.dot(contract_worths, weights, precision=lax.Precision.HIGHEST) / math.sqrt(SCENARIOS)
        dual_mass = jnp.sum(weights)
        holding_next = jnp.clip(holding - PRIMAL_STEP * gradient, -1.0, 1.0)
        level_next = level - THRESH_STEP * (1.0 - dual_mass / ((1.0 - TAIL_LEVEL) * SCENARIOS))
        holding_bar = 2.0 * holding_next - holding
        level_bar = 2.0 * level_next - level
        pnl = jnp.dot(holding_bar, contract_worths, precision=lax.Precision.HIGHEST) / math.sqrt(OPTIONS)
        weights = jnp.clip(weights + DUAL_STEP * (base_loss - pnl - level_bar), 0.0, 1.0)
        holding = holding_next
        level = level_next
    return (contract_worths, holding, weights, level.reshape(1))
```

```python
import math

import jax
import jax.numpy as jnp
from jax import lax
from jax.experimental import pallas as pl
from jax.experimental.pallas import tpu as pltpu
from jax.sharding import PartitionSpec as P

LOW_END = -4.0
HIGH_END = 4.0
TAIL_LEVEL = 0.9
PRIMAL_STEP = 0.5
THRESH_STEP = 0.05
DUAL_STEP = 0.5

LANES = 128
SCEN = 8
OPT = 16
DEVICES = SCEN * OPT
TERMS = 1024
SCENARIOS = 2048
OPTIONS = 16384
MOST = 2
CHUNKS = TERMS // LANES
BASE = 32
COEF_ROWS = CHUNKS + 1
MSG1 = MOST * COEF_ROWS + 2
MSG2 = MOST * 16 + 2
PAYLOAD = 24
ORDER = ("opt", "scen")
F32 = jnp.float32
BF16 = jnp.bfloat16
HIGHEST = lax.Precision.HIGHEST
NN = (((1,), (0,)), ((), ()))
NT = (((1,), (1,)), ((), ()))


def params():
    return pltpu.CompilerParams(vmem_limit_bytes=48 * 1024 * 1024)


def iota(shape, axis):
    return lax.broadcasted_iota(jnp.int32, shape, axis)


def owner_of(place):
    return (place & (SCEN - 1)) * OPT + (place >> 3)


def mm(a, b, dims=NN):
    return lax.dot_general(a, b, dims, preferred_element_type=F32)


def three(x):
    hi = x.astype(BF16)
    rest = x - hi.astype(F32)
    mid = rest.astype(BF16)
    low = (rest - mid.astype(F32)).astype(BF16)
    return hi, mid, low


def pick(onehot, x, dims=NN):
    hi, mid, low = three(x)
    return mm(onehot, hi, dims) + mm(onehot, mid, dims) + mm(onehot, low, dims)


def level_step(level, mass):
    return level - THRESH_STEP * (1.0 - mass / ((1.0 - TAIL_LEVEL) * SCENARIOS))


def primal(position, cost, gradient):
    return jnp.clip(
        position - PRIMAL_STEP * (cost - gradient / math.sqrt(SCENARIOS)), -1.0, 1.0
    )


def dual(weights, base, pnl, level_bar):
    return jnp.clip(
        weights + DUAL_STEP * (base - pnl / math.sqrt(OPTIONS) - level_bar), 0.0, 1.0
    )


def send_kernel(own_ref, coef_ref, cost_ref, pos_ref, dual_ref, out_ref):
    row = lax.axis_index("scen")
    square = (LANES, LANES)
    down, across = iota(square, 0), iota(square, 1)
    same = own_ref[pl.ds(row, 1), :] == owner_of(down)
    before = mm(
        same.astype(F32).astype(BF16), (down < across).astype(F32).astype(BF16)
    )
    cost = jnp.broadcast_to(cost_ref[pl.ds(row, 1), :], square)
    pos = jnp.broadcast_to(pos_ref[pl.ds(row, 1), :], square)
    pair = jnp.where(down == 0, cost, jnp.where(down == 1, pos, 0.0))
    for rank in range(MOST):
        chosen = jnp.where(same & (before == float(rank)), 1.0, 0.0).astype(BF16)
        for chunk in range(CHUNKS):
            out_ref[pl.ds(rank * COEF_ROWS + chunk, DEVICES, stride=MSG1), :] = pick(
                chosen, coef_ref[:, chunk * LANES : (chunk + 1) * LANES]
            )
        out_ref[pl.ds(rank * COEF_ROWS + CHUNKS, DEVICES, stride=MSG1), :] = pick(
            chosen, pair, NT
        )
    for half in range(2):
        out_ref[pl.ds(MSG1 - 2 + half, DEVICES, stride=MSG1), :] = jnp.broadcast_to(
            dual_ref[half : half + 1, :], square
        )


def turn(quarters, rest):
    x = rest * (2.0 * math.pi)
    z = x * x
    sin = x * (
        1.0 + z * (-1 / 6 + z * (1 / 120 + z * (-1 / 5040 + z * (1 / 362880))))
    )
    cos = 1.0 + z * (
        -1 / 2 + z * (1 / 24 + z * (-1 / 720 + z * (1 / 40320 - z * (1 / 3628800))))
    )
    swap = (quarters & 1) == 1
    cos_out = jnp.where(swap, sin, cos)
    sin_out = jnp.where(swap, cos, sin)
    cos_out = jnp.where(((quarters + 1) & 2) == 2, -cos_out, cos_out)
    sin_out = jnp.where((quarters & 2) == 2, -sin_out, sin_out)
    return cos_out, sin_out


def table_kernel(mean_ref, spread_ref, hi_ref, low_ref):
    width = mean_ref.shape[1]
    shape = (BASE, width)
    mean = mean_ref[...]
    coarse = jnp.round(mean * 2048.0) * (1.0 / 2048.0)
    fine = mean - coarse
    step = iota(shape, 0)
    stepf = step.astype(F32)

    def base(scale, extra):
        turns = (stepf * scale) * coarse
        quarters = jnp.round(turns * 4.0)
        rest = (turns - quarters * 0.25) + (stepf * scale) * fine
        return turn(quarters.astype(jnp.int32) + extra, rest)

    cos_b, sin_b = base(1.0 / 16.0, step)
    cos_a, sin_a = base(BASE / 16.0, jnp.zeros_like(step))
    cos_a, sin_a = cos_a * 0.25, sin_a * 0.25
    unit = math.pi / (HIGH_END - LOW_END)
    rate = spread_ref[...] * (-0.5 * unit * unit * math.log2(math.e))
    for a in range(BASE):
        k = stepf + float(BASE * a)
        decay = jnp.exp2((k * k) * rate)
        value = (cos_a[a : a + 1, :] * cos_b - sin_a[a : a + 1, :] * sin_b) * decay
        if a == 0:
            value = jnp.where(step == 0, value * 0.5, value)
        hi = value.astype(BF16)
        hi_ref[a * BASE : (a + 1) * BASE, :] = hi
        low_ref[a * BASE : (a + 1) * BASE, :] = (value - hi.astype(F32)).astype(BF16)


def value_kernel(
    in_ref, hi_ref, low_ref, out_ref, mass_ref, coef_hi, coef_low, values, grad
):
    block = pl.program_id(0)

    @pl.when(block == 0)
    def _():
        for rank in range(MOST):
            for chunk in range(CHUNKS):
                part = in_ref[pl.ds(rank * COEF_ROWS + chunk, DEVICES, stride=MSG1), :]
                hi = part.astype(BF16)
                at = (slice(rank * LANES, (rank + 1) * LANES), slice(chunk * LANES, (chunk + 1) * LANES))
                coef_hi[at] = hi
                coef_low[at] = (part - hi.astype(F32)).astype(BF16)
        grad[...] = jnp.zeros_like(grad)

    width = 2 * LANES
    table_hi = hi_ref[...]
    tile = (
        mm(coef_hi[...], table_hi)
        + mm(coef_hi[...], low_ref[...])
        + mm(coef_low[...], table_hi)
    )
    values[:, pl.ds(pl.multiple_of(block * width, width), width)] = tile
    first = in_ref[pl.ds(block * MSG1 + MSG1 - 2, 1), :]
    second = in_ref[pl.ds(block * MSG1 + MSG1 - 1, 1), :]
    grad[...] += tile[:, :LANES] * first + tile[:, LANES:] * second
    for o in range(OPT):
        for rank in range(MOST):
            for half in range(2):
                out_ref[
                    pl.ds((o * SCEN + block) * MSG2 + (rank * 2 + half) * 8, 8), :
                ] = tile[
                    rank * LANES + o * 8 : rank * LANES + o * 8 + 8,
                    half * LANES : (half + 1) * LANES,
                ]

    @pl.when(block == SCEN - 1)
    def _():
        mass = jnp.zeros((1, LANES), F32)
        for s in range(SCEN):
            for half in range(2):
                mass = mass + in_ref[s * MSG1 + MSG1 - 2 + half : s * MSG1 + MSG1 - 1 + half, :]
        mass_ref[0] = jnp.sum(mass)
        pnl = jnp.zeros((8, SCENARIOS), F32)
        for rank in range(MOST):
            extra = in_ref[pl.ds(rank * COEF_ROWS + CHUNKS, DEVICES, stride=MSG1), :]
            cost, pos = extra[:, 0:1], extra[:, 1:2]
            gradient = jnp.sum(grad[rank * LANES : (rank + 1) * LANES, :], axis=1, keepdims=True)
            bar = 2.0 * primal(pos, cost, gradient) - pos
            for group in range(LANES // 8):
                pnl = pnl + values[rank * LANES + group * 8 : rank * LANES + group * 8 + 8, :] * bar[group * 8 : group * 8 + 8, :]
        pnl = jnp.sum(pnl, axis=0, keepdims=True)
        for s in range(SCEN):
            for half in range(2):
                at = s * width + half * LANES
                out_ref[pl.ds(s * MSG2 + MSG2 - 2 + half, OPT, stride=SCEN * MSG2), :] = (
                    jnp.broadcast_to(pnl[:, at : at + LANES], (OPT, LANES))
                )


def tile_kernel(
    in_ref, own_ref, dual_ref, base_ref, mass_ref, level_ref, tile_ref, pay_ref, dual_out
):
    square = (LANES, LANES)
    down, across = iota(square, 0), iota(square, 1)
    level = level_ref[0]
    level_bar = 2.0 * level_step(level, mass_ref[0]) - level
    weights = []
    for half in range(2):
        pnl = jnp.sum(
            in_ref[pl.ds(MSG2 - 2 + half, DEVICES, stride=MSG2), :], axis=0, keepdims=True
        )
        weights.append(
            dual(dual_ref[half : half + 1, :], base_ref[half : half + 1, :], pnl, level_bar)
        )
        dual_out[half : half + 1, :] = weights[half]
    new = jnp.concatenate(weights, axis=1)
    old = jnp.concatenate([dual_ref[0:1, :], dual_ref[1:2, :]], axis=1)
    tall = iota((8, 2 * LANES), 0)
    both = jnp.where(
        tall == 0,
        jnp.broadcast_to(old, (8, 2 * LANES)),
        jnp.where(tall == 1, jnp.broadcast_to(new, (8, 2 * LANES)), 0.0),
    )
    names = jnp.concatenate([own_ref[...].astype(F32), jnp.zeros((LANES - SCEN, LANES), F32)], axis=0).T
    lower = (across < down).astype(F32).astype(BF16)
    owner = owner_of(across).astype(F32)
    rows = []
    for s in range(SCEN):
        same = names[:, s : s + 1] == owner
        before = mm(lower, same.astype(F32).astype(BF16))
        chosen = jnp.concatenate(
            [
                jnp.where(same & (before == float(rank)), 1.0, 0.0).astype(BF16)
                for rank in range(MOST)
            ],
            axis=1,
        )
        arrived = jnp.concatenate(
            [
                jnp.concatenate(
                    [
                        in_ref[pl.ds((rank * 2 + half) * 8 + s, DEVICES, stride=MSG2), :]
                        for half in range(2)
                    ],
                    axis=1,
                )
                for rank in range(MOST)
            ],
            axis=0,
        )
        tile = pick(chosen, arrived)
        tile_ref[s * LANES : (s + 1) * LANES, :] = tile
        rows.append(
            lax.dot_general(both, tile, NT, precision=HIGHEST, preferred_element_type=F32)
        )
    payload = jnp.concatenate(
        [r[0:1, :] for r in rows]
        + [r[1:2, :] for r in rows]
        + [weights[0] + weights[1], jnp.zeros((PAYLOAD - 17, LANES), F32)],
        axis=0,
    )
    for s in range(SCEN):
        pay_ref[s * PAYLOAD : (s + 1) * PAYLOAD, :] = payload


def position_kernel(
    in_ref, tile_ref, cost_ref, pos_ref, mass_ref, level_ref, pos_out, pnl_out, level_out, bar_out
):
    total = in_ref[0:PAYLOAD, :]
    for s in range(1, SCEN):
        total = total + in_ref[s * PAYLOAD : (s + 1) * PAYLOAD, :]
    level = level_step(level_ref[0], mass_ref[0])
    later = level_step(level, jnp.sum(total[16:17, :]))
    level_out[0] = later
    bar_out[0] = 2.0 * later - level
    cost = cost_ref[...]
    first = primal(pos_ref[...], cost, total[0:8, :])
    second = primal(first, cost, total[8:16, :])
    pos_out[...] = second
    bar = 2.0 * second - first
    pnl = jnp.zeros((1, 2 * LANES), F32)
    for s in range(SCEN):
        pnl = pnl + lax.dot_general(
            bar[s : s + 1, :],
            tile_ref[s * LANES : (s + 1) * LANES, :],
            NN,
            precision=HIGHEST,
            preferred_element_type=F32,
        )
    for o in range(OPT):
        for half in range(2):
            pnl_out[o * 2 + half : o * 2 + half + 1, :] = pnl[:, half * LANES : (half + 1) * LANES]


def dual_kernel(in_ref, dual_ref, base_ref, bar_ref, out_ref):
    pnl = in_ref[0:2, :]
    for o in range(1, OPT):
        pnl = pnl + in_ref[2 * o : 2 * o + 2, :]
    out_ref[...] = dual(dual_ref[...], base_ref[...], pnl, bar_ref[0])


VMEM = pl.BlockSpec(memory_space=pltpu.VMEM)
SMEM = pl.BlockSpec(memory_space=pltpu.SMEM)


def exchange(x, axes):
    return lax.all_to_all(x, axes, split_axis=0, concat_axis=0, tiled=True)


def shaped(*shape, dtype=F32):
    return jax.ShapeDtypeStruct(shape, dtype)


def on_device(
    option_coefs,
    underlying_of,
    log_return_mean,
    log_return_spread,
    cost,
    positions,
    base_loss,
    duals,
    threshold,
):
    own = underlying_of.reshape(SCEN, LANES)
    cost = cost.reshape(SCEN, LANES)
    positions = positions.reshape(SCEN, LANES)
    base_loss = base_loss.reshape(2, LANES)
    duals = duals.reshape(2, LANES)

    sent = pl.pallas_call(
        send_kernel,
        out_shape=shaped(DEVICES * MSG1, LANES),
        in_specs=[VMEM] * 5,
        out_specs=VMEM,
        compiler_params=params(),
    )(own, option_coefs, cost, positions, duals)
    got = exchange(sent.reshape(DEVICES, MSG1 // 2, 2, LANES), ORDER)
    got = got.reshape(DEVICES * MSG1, LANES)

    width = 2 * LANES
    row = pl.BlockSpec((1, width), lambda i: (0, i))
    column = pl.BlockSpec((TERMS, width), lambda i: (0, i))
    table_hi, table_low = pl.pallas_call(
        table_kernel,
        grid=(SCENARIOS // width,),
        out_shape=[shaped(TERMS, SCENARIOS, dtype=BF16)] * 2,
        in_specs=[row, row],
        out_specs=[column, column],
        compiler_params=params(),
        cost_estimate=pl.CostEstimate(
            flops=20 * TERMS * SCENARIOS,
            bytes_accessed=4 * TERMS * SCENARIOS,
            transcendentals=TERMS * SCENARIOS,
        ),
    )(log_return_mean, log_return_spread)

    whole = lambda rows: pl.BlockSpec((rows, LANES), lambda i: (0, 0))
    values, mass = pl.pallas_call(
        value_kernel,
        grid=(SCENARIOS // width,),
        out_shape=[shaped(DEVICES * MSG2, LANES), shaped(1)],
        in_specs=[whole(DEVICES * MSG1), column, column],
        out_specs=[whole(DEVICES * MSG2), SMEM],
        scratch_shapes=[
            pltpu.VMEM((MOST * LANES, TERMS), BF16),
            pltpu.VMEM((MOST * LANES, TERMS), BF16),
            pltpu.VMEM((MOST * LANES, SCENARIOS), F32),
            pltpu.VMEM((MOST * LANES, LANES), F32),
        ],
        compiler_params=params(),
    )(got, table_hi, table_low)
    arrived = exchange(values.reshape(DEVICES, MSG2 // 2, 2, LANES), ORDER)
    arrived = arrived.reshape(DEVICES * MSG2, LANES)

    tile, payload, first_duals = pl.pallas_call(
        tile_kernel,
        out_shape=[
            shaped(SCEN * LANES, width),
            shaped(SCEN * PAYLOAD, LANES),
            shaped(2, LANES),
        ],
        in_specs=[VMEM] * 4 + [SMEM] * 2,
        out_specs=[VMEM] * 3,
        compiler_params=params(),
    )(arrived, own, duals, base_loss, mass, threshold)
    gathered = exchange(payload.reshape(SCEN, PAYLOAD, LANES), "scen")

    new_positions, part_pnl, level, level_bar = pl.pallas_call(
        position_kernel,
        out_shape=[shaped(SCEN, LANES), shaped(OPT * 2, LANES), shaped(1), shaped(1)],
        in_specs=[VMEM] * 4 + [SMEM] * 2,
        out_specs=[VMEM] * 2 + [SMEM] * 2,
        compiler_params=params(),
    )(gathered.reshape(SCEN * PAYLOAD, LANES), tile, cost, positions, mass, threshold)
    pnl = exchange(part_pnl.reshape(OPT, 2, LANES), "opt")

    new_duals = pl.pallas_call(
        dual_kernel,
        out_shape=shaped(2, LANES),
        in_specs=[VMEM] * 3 + [SMEM],
        out_specs=VMEM,
        compiler_params=params(),
    )(pnl.reshape(OPT * 2, LANES), first_duals, base_loss, level_bar)
    return (tile, new_positions.reshape(-1), new_duals.reshape(-1), level)


def solution(mesh):
    in_specs = (
        P(("opt", "scen"), None),
        P("opt", None),
        P(("scen", "opt"), None),
        P(("scen", "opt"), None),
        P("opt"),
        P("opt"),
        P("scen"),
        P("scen"),
        P(),
    )
    out_specs = (P("opt", "scen"), P("opt"), P("scen"), P())
    return jax.shard_map(
        on_device, mesh=mesh, in_specs=in_specs, out_specs=out_specs, check_vma=False
    )
```

```python
import math

import jax
import jax.numpy as jnp
from jax import lax
from jax.experimental import pallas as pl
from jax.experimental.pallas import tpu as pltpu
from jax.sharding import PartitionSpec as P

LOW_END = -4.0
HIGH_END = 4.0
TAIL_LEVEL = 0.9
PRIMAL_STEP = 0.5
THRESH_STEP = 0.05
DUAL_STEP = 0.5

LANES = 128
SCEN = 8
OPT = 16
DEVICES = SCEN * OPT
TERMS = 1024
SCENARIOS = 2048
OPTIONS = 16384
MOST = 2
CHUNKS = TERMS // LANES
BASE = 32
TABLE = 512
BLOCKS = SCENARIOS // TABLE
READY = 2
BASE_ROWS = 4 * BASE + 8
PAIR = MOST * CHUNKS
DUAL = PAIR + 1
MSG1 = PAIR + 2
MSG2 = MOST * 16 + 2
PAYLOAD = 24
PARTS = 4
ORDER = ("opt", "scen")
F32 = jnp.float32
BF16 = jnp.bfloat16
HIGHEST = lax.Precision.HIGHEST
NN = (((1,), (0,)), ((), ()))
NT = (((1,), (1,)), ((), ()))


def params(mib):
    return pltpu.CompilerParams(vmem_limit_bytes=int(mib * 1024 * 1024))


def iota(shape, axis):
    return lax.broadcasted_iota(jnp.int32, shape, axis)


def owner_of(place):
    return (place & (SCEN - 1)) * OPT + (place >> 3)


def mm(a, b, dims=NN):
    return lax.dot_general(a, b, dims, preferred_element_type=F32)


def three(x):
    hi = x.astype(BF16)
    rest = x - hi.astype(F32)
    mid = rest.astype(BF16)
    low = (rest - mid.astype(F32)).astype(BF16)
    return hi, mid, low


def pick(onehot, x, dims=NN):
    hi, mid, low = three(x)
    return mm(onehot, hi, dims) + mm(onehot, mid, dims) + mm(onehot, low, dims)


def level_step(level, mass):
    return level - THRESH_STEP * (1.0 - mass / ((1.0 - TAIL_LEVEL) * SCENARIOS))


def primal(position, cost, gradient):
    return jnp.clip(
        position - PRIMAL_STEP * (cost - gradient / math.sqrt(SCENARIOS)), -1.0, 1.0
    )


def dual(weights, base, pnl, level_bar):
    return jnp.clip(
        weights + DUAL_STEP * (base - pnl / math.sqrt(OPTIONS) - level_bar), 0.0, 1.0
    )


def send_kernel(
    own_hbm, coef_hbm, cost_hbm, pos_hbm, dual_hbm, out_hbm,
    own_ref, coef_ref, cost_ref, pos_ref, dual_ref, out_ref, sems, out_sems,
):
    pairs = (
        (own_hbm, own_ref),
        (cost_hbm, cost_ref),
        (pos_hbm, pos_ref),
        (dual_hbm, dual_ref),
        (coef_hbm, coef_ref),
    )
    copies = [pltpu.make_async_copy(a, b, sems.at[i]) for i, (a, b) in enumerate(pairs)]
    for copy in copies:
        copy.start()
    for copy in copies[:4]:
        copy.wait()
    row = lax.axis_index("scen")
    half = lax.axis_index("opt") & 1
    square = (LANES, LANES)
    down, across = iota(square, 0), iota(square, 1)
    same = own_ref[pl.ds(row, 1), :] == owner_of(down)
    before = mm(
        same.astype(F32).astype(BF16), (down < across).astype(F32).astype(BF16)
    )
    cost = jnp.broadcast_to(cost_ref[pl.ds(row, 1), :], square)
    pos = jnp.broadcast_to(pos_ref[pl.ds(row, 1), :], square)
    chosen = [
        jnp.where(same & (before == float(rank)), 1.0, 0.0).astype(BF16)
        for rank in range(MOST)
    ]
    pair = jnp.zeros(square, F32)
    for rank in range(MOST):
        packed = jnp.where(
            down == 2 * rank, cost, jnp.where(down == 2 * rank + 1, pos, 0.0)
        )
        pair = pair + pick(chosen[rank], packed, NT)
    out_ref[pl.ds(PAIR, DEVICES, stride=MSG1), :] = pair
    out_ref[pl.ds(DUAL, DEVICES, stride=MSG1), :] = jnp.broadcast_to(
        dual_ref[pl.ds(half, 1), :], square
    )
    copies[4].wait()
    hi, mid, low = three(coef_ref[...])
    size = DEVICES // PARTS
    outs = []
    for part in range(PARTS):
        for rank in range(MOST):
            some = chosen[rank][part * size : (part + 1) * size, :]
            rows = mm(some, hi) + mm(some, mid) + mm(some, low)
            for chunk in range(CHUNKS):
                start = part * size * MSG1 + rank * CHUNKS + chunk
                out_ref[pl.ds(start, size, stride=MSG1), :] = rows[
                    :, chunk * LANES : (chunk + 1) * LANES
                ]
        at = slice(part * size * MSG1, (part + 1) * size * MSG1)
        outs.append(
            pltpu.make_async_copy(out_ref.at[at], out_hbm.at[at], out_sems.at[part])
        )
        outs[part].start()
    for out in outs:
        out.wait()


def turn(quarters, rest):
    x = rest * (2.0 * math.pi)
    z = x * x
    sin = x * (
        1.0 + z * (-1 / 6 + z * (1 / 120 + z * (-1 / 5040 + z * (1 / 362880))))
    )
    cos = 1.0 + z * (
        -1 / 2 + z * (1 / 24 + z * (-1 / 720 + z * (1 / 40320 - z * (1 / 3628800))))
    )
    swap = (quarters & 1) == 1
    cos_out = jnp.where(swap, sin, cos)
    sin_out = jnp.where(swap, cos, sin)
    cos_out = jnp.where(((quarters + 1) & 2) == 2, -cos_out, cos_out)
    sin_out = jnp.where((quarters & 2) == 2, -sin_out, sin_out)
    return cos_out, sin_out


def base_kernel(mean_ref, spread_ref, out_ref, hi_ref, low_ref):
    shape = (BASE, TABLE)
    mean = mean_ref[...]
    coarse = jnp.round(mean * 2048.0) * (1.0 / 2048.0)
    fine = mean - coarse
    step = iota(shape, 0)
    stepf = step.astype(F32)

    def base(scale, extra):
        turns = (stepf * scale) * coarse
        quarters = jnp.round(turns * 4.0)
        rest = (turns - quarters * 0.25) + (stepf * scale) * fine
        return turn(quarters.astype(jnp.int32) + extra, rest)

    cos_b, sin_b = base(1.0 / 16.0, step)
    cos_a, sin_a = base(BASE / 16.0, jnp.zeros_like(step))
    unit = math.pi / (HIGH_END - LOW_END)
    rate = spread_ref[...] * (-0.5 * unit * unit * math.log2(math.e))
    out_ref[0, 0:BASE, :] = cos_a * 0.25
    out_ref[0, BASE : 2 * BASE, :] = sin_a * 0.25
    out_ref[0, 2 * BASE : 3 * BASE, :] = cos_b
    out_ref[0, 3 * BASE : 4 * BASE, :] = sin_b
    out_ref[0, 4 * BASE :, :] = jnp.broadcast_to(rate, (8, TABLE))

    @pl.when(pl.program_id(0) < READY)
    def _():
        table(out_ref.at[0], hi_ref.at[0], low_ref.at[0])


def choice_kernel(own_ref, out_ref):
    square = (LANES, LANES)
    down, across = iota(square, 0), iota(square, 1)
    names = jnp.concatenate(
        [own_ref[...].astype(F32), jnp.zeros((LANES - SCEN, LANES), F32)], axis=0
    ).T
    lower = (across < down).astype(F32).astype(BF16)
    owner = across.astype(F32)
    for s in range(SCEN):
        same = names[:, s : s + 1] == owner
        before = mm(lower, same.astype(F32).astype(BF16))
        for rank in range(MOST):
            out_ref[s, :, rank * LANES : (rank + 1) * LANES] = jnp.where(
                same & (before == float(rank)), 1.0, 0.0
            ).astype(BF16)


def table(base_ref, hi_ref, low_ref):
    step = iota((BASE, LANES), 0)
    stepf = step.astype(F32)
    for half in range(TABLE // LANES):
        at = slice(half * LANES, (half + 1) * LANES)
        cos_b = base_ref[2 * BASE : 3 * BASE, at]
        sin_b = base_ref[3 * BASE : 4 * BASE, at]
        rate = base_ref[4 * BASE : 4 * BASE + 1, at]
        for a in range(BASE):
            k = stepf + float(BASE * a)
            value = (
                base_ref[a : a + 1, at] * cos_b
                - base_ref[BASE + a : BASE + a + 1, at] * sin_b
            ) * jnp.exp2((k * k) * rate)
            if a == 0:
                value = jnp.where(step == 0, value * 0.5, value)
            hi = value.astype(BF16)
            hi_ref[a * BASE : (a + 1) * BASE, at] = hi
            low_ref[a * BASE : (a + 1) * BASE, at] = (value - hi.astype(F32)).astype(BF16)


def value_kernel(
    in_hbm, base_hbm, hi_hbm, low_hbm, out_hbm, mass_ref,
    in_ref, base_ref, hi_0, low_0, hi_1, low_1, hi_made, low_made, coef, values, grad, out_ref, sems, out_sems,
):
    width = 2 * LANES
    rows = MOST * LANES
    firsts = [
        pltpu.make_async_copy(base_hbm.at[READY], base_ref.at[0], sems.at[2, 0]),
        pltpu.make_async_copy(in_hbm, in_ref, sems.at[2, 1]),
        pltpu.make_async_copy(base_hbm.at[READY + 1], base_ref.at[1], sems.at[3, 0]),
    ]
    for copy in firsts:
        copy.start()
    copies = [
        (
            pltpu.make_async_copy(hi_hbm.at[block], hi_made.at[block], sems.at[0, block]),
            pltpu.make_async_copy(low_hbm.at[block], low_made.at[block], sems.at[1, block]),
        )
        for block in range(READY)
    ]
    for pair in copies:
        for copy in pair:
            copy.start()
    firsts[0].wait()
    table(base_ref.at[0], hi_0, low_0)
    firsts[1].wait()
    for rank in range(MOST):
        for chunk in range(CHUNKS):
            part = in_ref[pl.ds(rank * CHUNKS + chunk, DEVICES, stride=MSG1), :]
            hi = part.astype(BF16)
            at = slice(chunk * LANES, (chunk + 1) * LANES)
            coef[rank * LANES : (rank + 1) * LANES, at] = hi
            coef[rows + rank * LANES : rows + (rank + 1) * LANES, at] = (
                part - hi.astype(F32)
            ).astype(BF16)
    grad[...] = jnp.zeros_like(grad)
    firsts[2].wait()

    def multiply(block, hi_ref, low_ref):
        both = mm(coef[...], hi_ref[...])
        wide = both[:rows] + both[rows:] + mm(coef[:rows, :], low_ref[...])
        total = grad[...]
        for part in range(TABLE // width):
            s = block * (TABLE // width) + part
            tile = wide[:, part * width : (part + 1) * width]
            values[s] = tile
            for half in range(2):
                weights = in_ref[pl.ds((half * SCEN + s) * MSG1 + DUAL, 1), :]
                total = total + tile[:, half * LANES : (half + 1) * LANES] * weights
            start = s * OPT * MSG2
            for o in range(OPT):
                for rank in range(MOST):
                    for half in range(2):
                        out_ref[
                            pl.ds(start + o * MSG2 + (rank * 2 + half) * 8, 8), :
                        ] = tile[
                            rank * LANES + o * 8 : rank * LANES + o * 8 + 8,
                            half * LANES : (half + 1) * LANES,
                        ]
        grad[...] = total

    tiles = out_ref.reshape(DEVICES // 4, 17, 8, LANES)
    outs = []

    def send(*view):
        outs.append(
            pltpu.make_async_copy(tiles.at[view], out_hbm.at[view], out_sems.at[len(outs)])
        )
        outs[-1].start()

    def send_values(block):
        share = DEVICES // 4 // BLOCKS
        for first, last in ((0, 4), (5, 8), (9, 12), (13, 16)):
            send(slice(block * share, (block + 1) * share), slice(first, last))

    multiply(READY, hi_0, low_0)
    send_values(READY)
    table(base_ref.at[1], hi_1, low_1)
    multiply(READY + 1, hi_1, low_1)
    send_values(READY + 1)
    for block in range(READY):
        for copy in copies[block]:
            copy.wait()
        multiply(block, hi_made.at[block], low_made.at[block])
        send_values(block)

    mass = jnp.zeros((1, LANES), F32)
    for place in range(2 * SCEN):
        at = place * MSG1 + DUAL
        mass = mass + in_ref[at : at + 1, :]
    mass_ref[0] = jnp.sum(mass)
    extra = in_ref[pl.ds(PAIR, DEVICES, stride=MSG1), :]
    bars = []
    for rank in range(MOST):
        cost, pos = extra[:, 2 * rank : 2 * rank + 1], extra[:, 2 * rank + 1 : 2 * rank + 2]
        gradient = jnp.sum(
            grad[rank * LANES : (rank + 1) * LANES, :], axis=1, keepdims=True
        )
        bars.append(2.0 * primal(pos, cost, gradient) - pos)
    bar = jnp.broadcast_to(jnp.concatenate(bars, axis=0), (rows, LANES))
    for s in range(SCEN):
        for half in range(2):
            pnl = values[s, :, half * LANES : (half + 1) * LANES] * bar
            out_ref[pl.ds(s * OPT * MSG2 + MSG2 - 2 + half, OPT, stride=MSG2), :] = (
                jnp.broadcast_to(jnp.sum(pnl, axis=0, keepdims=True), (OPT, LANES))
            )
    for tile in (4, 8, 12, 16):
        send(slice(0, DEVICES // 4), slice(tile, tile + 1))
    for out in outs:
        out.wait()


def tile_kernel(
    in_ref, choice_ref, dual_ref, base_ref, mass_ref, level_ref, tile_ref, pay_ref, dual_out
):
    level = level_ref[0]
    level_bar = 2.0 * level_step(level, mass_ref[0]) - level
    weights = []
    for half in range(2):
        pnl = jnp.sum(
            in_ref[pl.ds(MSG2 - 2 + half, DEVICES, stride=MSG2), :], axis=0, keepdims=True
        )
        weights.append(
            dual(dual_ref[half : half + 1, :], base_ref[half : half + 1, :], pnl, level_bar)
        )
        dual_out[half : half + 1, :] = weights[half]
    new = jnp.concatenate(weights, axis=1)
    old = jnp.concatenate([dual_ref[0:1, :], dual_ref[1:2, :]], axis=1)
    tall = iota((8, 2 * LANES), 0)
    both = jnp.where(
        tall == 0,
        jnp.broadcast_to(old, (8, 2 * LANES)),
        jnp.where(tall == 1, jnp.broadcast_to(new, (8, 2 * LANES)), 0.0),
    )
    rows = []
    for s in range(SCEN):
        arrived = jnp.concatenate(
            [
                jnp.concatenate(
                    [
                        in_ref[pl.ds((rank * 2 + half) * 8 + s, DEVICES, stride=MSG2), :]
                        for half in range(2)
                    ],
                    axis=1,
                )
                for rank in range(MOST)
            ],
            axis=0,
        )
        tile = pick(choice_ref[s], arrived)
        tile_ref[s * LANES : (s + 1) * LANES, :] = tile
        rows.append(
            lax.dot_general(both, tile, NT, precision=HIGHEST, preferred_element_type=F32)
        )
    payload = jnp.concatenate(
        [r[0:1, :] for r in rows]
        + [r[1:2, :] for r in rows]
        + [weights[0] + weights[1], jnp.zeros((PAYLOAD - 17, LANES), F32)],
        axis=0,
    )
    for s in range(SCEN):
        pay_ref[s * PAYLOAD : (s + 1) * PAYLOAD, :] = payload


def position_kernel(
    in_ref, tile_ref, cost_ref, pos_ref, mass_ref, level_ref,
    pos_out, pnl_out, tile_hbm, level_out, bar_out, sem,
):
    keep = pltpu.make_async_copy(tile_ref, tile_hbm, sem)
    keep.start()
    total = in_ref[0:PAYLOAD, :]
    for s in range(1, SCEN):
        total = total + in_ref[s * PAYLOAD : (s + 1) * PAYLOAD, :]
    level = level_step(level_ref[0], mass_ref[0])
    later = level_step(level, jnp.sum(total[16:17, :]))
    level_out[0] = later
    bar_out[0] = 2.0 * later - level
    cost = cost_ref[...]
    first = primal(pos_ref[...], cost, total[0:8, :])
    second = primal(first, cost, total[8:16, :])
    pos_out[...] = second
    bar = 2.0 * second - first
    pnl = jnp.zeros((1, 2 * LANES), F32)
    for s in range(SCEN):
        pnl = pnl + lax.dot_general(
            bar[s : s + 1, :],
            tile_ref[s * LANES : (s + 1) * LANES, :],
            NN,
            precision=HIGHEST,
            preferred_element_type=F32,
        )
    for o in range(OPT):
        for half in range(2):
            pnl_out[o * 2 + half : o * 2 + half + 1, :] = pnl[:, half * LANES : (half + 1) * LANES]
    keep.wait()


def dual_kernel(in_ref, dual_ref, base_ref, bar_ref, out_ref):
    pnl = in_ref[0:2, :]
    for o in range(1, OPT):
        pnl = pnl + in_ref[2 * o : 2 * o + 2, :]
    out_ref[...] = dual(dual_ref[...], base_ref[...], pnl, bar_ref[0])


VMEM = pl.BlockSpec(memory_space=pltpu.VMEM)
HBM = pl.BlockSpec(memory_space=pltpu.HBM)
SMEM = pl.BlockSpec(memory_space=pltpu.SMEM)


def exchange(x, axes):
    return lax.all_to_all(x, axes, split_axis=0, concat_axis=0, tiled=True)


def shaped(*shape, dtype=F32):
    return jax.ShapeDtypeStruct(shape, dtype)


def value_scratch():
    return [
        pltpu.VMEM((DEVICES * MSG1, LANES), F32),
        pltpu.VMEM((BLOCKS - READY, BASE_ROWS, TABLE), F32),
        *[pltpu.VMEM((TERMS, TABLE), BF16)] * 4,
        *[pltpu.VMEM((READY, TERMS, TABLE), BF16)] * 2,
        pltpu.VMEM((2 * MOST * LANES, TERMS), BF16),
        pltpu.VMEM((SCEN, MOST * LANES, 2 * LANES), F32),
        pltpu.VMEM((MOST * LANES, LANES), F32),
        pltpu.VMEM((DEVICES * MSG2, LANES), F32),
        pltpu.SemaphoreType.DMA((4, 2)),
        pltpu.SemaphoreType.DMA((4 * BLOCKS + 4,)),
    ]


def on_device(
    option_coefs,
    underlying_of,
    log_return_mean,
    log_return_spread,
    cost,
    positions,
    base_loss,
    duals,
    threshold,
):
    own = underlying_of.reshape(SCEN, LANES)
    cost = cost.reshape(SCEN, LANES)
    positions = positions.reshape(SCEN, LANES)
    base_loss = base_loss.reshape(2, LANES)
    duals = duals.reshape(2, LANES)

    sent = pl.pallas_call(
        send_kernel,
        out_shape=shaped(DEVICES * MSG1, LANES),
        in_specs=[HBM] * 5,
        out_specs=HBM,
        scratch_shapes=[
            pltpu.VMEM((SCEN, LANES), jnp.int32),
            pltpu.VMEM((LANES, TERMS), F32),
            pltpu.VMEM((SCEN, LANES), F32),
            pltpu.VMEM((SCEN, LANES), F32),
            pltpu.VMEM((2, LANES), F32),
            pltpu.VMEM((DEVICES * MSG1, LANES), F32),
            pltpu.SemaphoreType.DMA((5,)),
            pltpu.SemaphoreType.DMA((PARTS,)),
        ],
        compiler_params=params(63),
    )(own, option_coefs, cost, positions, duals)
    got = exchange(sent.reshape(DEVICES, MSG1 // 2, 2, LANES), ORDER)
    got = got.reshape(DEVICES * MSG1, LANES)

    made = pl.BlockSpec((1, TERMS, TABLE), lambda i: (jnp.minimum(i, READY - 1), 0, 0))
    base, made_hi, made_low = pl.pallas_call(
        base_kernel,
        grid=(BLOCKS,),
        out_shape=[
            pltpu.HBM((BLOCKS, BASE_ROWS, TABLE), F32),
            *[pltpu.HBM((READY, TERMS, TABLE), BF16)] * 2,
        ],
        in_specs=[pl.BlockSpec((1, TABLE), lambda i: (0, i))] * 2,
        out_specs=[pl.BlockSpec((1, BASE_ROWS, TABLE), lambda i: (i, 0, 0)), made, made],
        compiler_params=params(12),
        cost_estimate=pl.CostEstimate(
            flops=2 * TERMS * SCENARIOS,
            bytes_accessed=TERMS * SCENARIOS,
            transcendentals=0,
        ),
    )(log_return_mean, log_return_spread)
    choice = pl.pallas_call(
        choice_kernel,
        out_shape=shaped(SCEN, LANES, MOST * LANES, dtype=BF16),
        in_specs=[VMEM],
        out_specs=VMEM,
        compiler_params=params(4),
        cost_estimate=pl.CostEstimate(
            flops=TERMS * SCENARIOS, bytes_accessed=SCENARIOS, transcendentals=0
        ),
    )(own)

    values, mass = pl.pallas_call(
        value_kernel,
        out_shape=[shaped(DEVICES // 4, 17, 8, LANES), shaped(1)],
        in_specs=[HBM] * 4,
        out_specs=[HBM, SMEM],
        scratch_shapes=value_scratch(),
        compiler_params=params(63),
    )(got, base, made_hi, made_low)
    arrived = exchange(values.reshape(DEVICES, MSG2 // 2, 2, LANES), ("scen", "opt"))
    arrived = arrived.reshape(DEVICES * MSG2, LANES)

    tile, payload, first_duals = pl.pallas_call(
        tile_kernel,
        out_shape=[
            shaped(SCEN * LANES, 2 * LANES),
            shaped(SCEN * PAYLOAD, LANES),
            shaped(2, LANES),
        ],
        in_specs=[VMEM] * 4 + [SMEM] * 2,
        out_specs=[VMEM] * 3,
        compiler_params=params(12),
    )(arrived, choice, duals, base_loss, mass, threshold)
    gathered = exchange(payload.reshape(SCEN, PAYLOAD, LANES), "scen")

    new_positions, part_pnl, kept, level, level_bar = pl.pallas_call(
        position_kernel,
        out_shape=[
            shaped(SCEN, LANES),
            shaped(OPT * 2, LANES),
            shaped(SCEN * LANES, 2 * LANES),
            shaped(1),
            shaped(1),
        ],
        in_specs=[VMEM] * 4 + [SMEM] * 2,
        out_specs=[VMEM] * 2 + [HBM] + [SMEM] * 2,
        scratch_shapes=[pltpu.SemaphoreType.DMA(())],
        compiler_params=params(8),
    )(gathered.reshape(SCEN * PAYLOAD, LANES), tile, cost, positions, mass, threshold)
    pnl = exchange(part_pnl.reshape(OPT, 2, LANES), "opt")

    new_duals = pl.pallas_call(
        dual_kernel,
        out_shape=shaped(2, LANES),
        in_specs=[VMEM] * 3 + [SMEM],
        out_specs=VMEM,
        compiler_params=params(8),
    )(pnl.reshape(OPT * 2, LANES), first_duals, base_loss, level_bar)
    return (kept, new_positions.reshape(-1), new_duals.reshape(-1), level)


def solution(mesh):
    in_specs = (
        P(("opt", "scen"), None),
        P("opt", None),
        P(("scen", "opt"), None),
        P(("scen", "opt"), None),
        P("opt"),
        P("opt"),
        P("scen"),
        P("scen"),
        P(),
    )
    out_specs = (P("opt", "scen"), P("opt"), P("scen"), P())
    return jax.shard_map(
        on_device, mesh=mesh, in_specs=in_specs, out_specs=out_specs, check_vma=False
    )
```

```python
import math

import jax
import jax.numpy as jnp
from jax import lax
from jax.experimental import pallas as pl
from jax.experimental.pallas import tpu as pltpu
from jax.sharding import PartitionSpec as P

LOW_END = -4.0
HIGH_END = 4.0
TAIL_LEVEL = 0.9
PRIMAL_STEP = 0.5
THRESH_STEP = 0.05
DUAL_STEP = 0.5

LANES = 128
SCEN = 8
OPT = 16
DEVICES = SCEN * OPT
TERMS = 1024
SCENARIOS = 2048
OPTIONS = 16384
MOST = 2
CHUNKS = TERMS // LANES
BASE = 32
TABLE = 512
BLOCKS = SCENARIOS // TABLE
READY = 2
BASE_ROWS = 4 * BASE + 8
PAIR = MOST * CHUNKS
DUAL = PAIR + 1
MSG1 = PAIR + 2
MSG2 = MOST * 16 + 2
PAYLOAD = 24
PARTS = 4
STORED = 5
AXES = ("z_lo", "x", "z_hi", "y", "core")
SIZES = (2, 4, 2, 4, 2)
SCEN_AXES, OPT_AXES = AXES[:2], AXES[2:]
F32 = jnp.float32
BF16 = jnp.bfloat16
HIGHEST = lax.Precision.HIGHEST
NN = (((1,), (0,)), ((), ()))
NT = (((1,), (1,)), ((), ()))


def params(mib):
    return pltpu.CompilerParams(vmem_limit_bytes=int(mib * 1024 * 1024))


def iota(shape, axis):
    return lax.broadcasted_iota(jnp.int32, shape, axis)


def owner_of(place):
    return (place & (SCEN - 1)) * OPT + (place >> 3)


def mm(a, b, dims=NN):
    return lax.dot_general(a, b, dims, preferred_element_type=F32)


def three(x):
    hi = x.astype(BF16)
    rest = x - hi.astype(F32)
    mid = rest.astype(BF16)
    low = (rest - mid.astype(F32)).astype(BF16)
    return hi, mid, low


def two(x):
    hi = x.astype(BF16)
    return hi, (x - hi.astype(F32)).astype(BF16)


def pick(onehot, x, dims=NN):
    hi, mid, low = three(x)
    return mm(onehot, hi, dims) + mm(onehot, mid, dims) + mm(onehot, low, dims)


def level_step(level, mass):
    return level - THRESH_STEP * (1.0 - mass / ((1.0 - TAIL_LEVEL) * SCENARIOS))


def primal(position, cost, gradient):
    return jnp.clip(
        position - PRIMAL_STEP * (cost - gradient / math.sqrt(SCENARIOS)), -1.0, 1.0
    )


def dual(weights, base, pnl, level_bar):
    return jnp.clip(
        weights + DUAL_STEP * (base - pnl / math.sqrt(OPTIONS) - level_bar), 0.0, 1.0
    )


def send_kernel(
    own_hbm, coef_hbm, cost_hbm, pos_hbm, dual_hbm, out_hbm,
    own_ref, coef_ref, cost_ref, pos_ref, dual_ref, out_ref, sems, out_sems,
):
    pairs = (
        (own_hbm, own_ref),
        (cost_hbm, cost_ref),
        (pos_hbm, pos_ref),
        (dual_hbm, dual_ref),
        (coef_hbm, coef_ref),
    )
    copies = [pltpu.make_async_copy(a, b, sems.at[i]) for i, (a, b) in enumerate(pairs)]
    for copy in copies:
        copy.start()
    for copy in copies[:4]:
        copy.wait()
    row = lax.axis_index("z_lo") * 4 + lax.axis_index("x")
    half = lax.axis_index("core")
    square = (LANES, LANES)
    down, across = iota(square, 0), iota(square, 1)
    same = own_ref[pl.ds(row, 1), :] == owner_of(down)
    before = mm(
        same.astype(F32).astype(BF16), (down < across).astype(F32).astype(BF16)
    )
    cost = jnp.broadcast_to(cost_ref[pl.ds(row, 1), :], square)
    pos = jnp.broadcast_to(pos_ref[pl.ds(row, 1), :], square)
    chosen = [
        jnp.where(same & (before == float(rank)), 1.0, 0.0).astype(BF16)
        for rank in range(MOST)
    ]
    pair = jnp.zeros(square, F32)
    for rank in range(MOST):
        packed = jnp.where(
            down == 2 * rank, cost, jnp.where(down == 2 * rank + 1, pos, 0.0)
        )
        pair = pair + pick(chosen[rank], packed, NT)
    out_ref[pl.ds(PAIR, DEVICES, stride=MSG1), :] = pair
    out_ref[pl.ds(DUAL, DEVICES, stride=MSG1), :] = jnp.broadcast_to(
        dual_ref[pl.ds(half, 1), :], square
    )
    copies[4].wait()
    hi, mid = two(coef_ref[...])
    size = DEVICES // PARTS
    outs = []
    for part in range(PARTS):
        for rank in range(MOST):
            some = chosen[rank][part * size : (part + 1) * size, :]
            rows = mm(some, hi) + mm(some, mid)
            for chunk in range(CHUNKS):
                start = part * size * MSG1 + rank * CHUNKS + chunk
                out_ref[pl.ds(start, size, stride=MSG1), :] = rows[
                    :, chunk * LANES : (chunk + 1) * LANES
                ]
        at = slice(part * size * MSG1, (part + 1) * size * MSG1)
        outs.append(
            pltpu.make_async_copy(out_ref.at[at], out_hbm.at[at], out_sems.at[part])
        )
        outs[part].start()
    for out in outs:
        out.wait()


def turn(quarters, rest):
    x = rest * (2.0 * math.pi)
    z = x * x
    sin = x * (
        1.0 + z * (-1 / 6 + z * (1 / 120 + z * (-1 / 5040 + z * (1 / 362880))))
    )
    cos = 1.0 + z * (
        -1 / 2 + z * (1 / 24 + z * (-1 / 720 + z * (1 / 40320 - z * (1 / 3628800))))
    )
    swap = (quarters & 1) == 1
    cos_out = jnp.where(swap, sin, cos)
    sin_out = jnp.where(swap, cos, sin)
    cos_out = jnp.where(((quarters + 1) & 2) == 2, -cos_out, cos_out)
    sin_out = jnp.where((quarters & 2) == 2, -sin_out, sin_out)
    return cos_out, sin_out


def base_kernel(mean_ref, spread_ref, out_ref, hi_ref, low_ref):
    shape = (BASE, TABLE)
    mean = mean_ref[...]
    coarse = jnp.round(mean * 2048.0) * (1.0 / 2048.0)
    fine = mean - coarse
    step = iota(shape, 0)
    stepf = step.astype(F32)

    def base(scale, extra):
        turns = (stepf * scale) * coarse
        quarters = jnp.round(turns * 4.0)
        rest = (turns - quarters * 0.25) + (stepf * scale) * fine
        return turn(quarters.astype(jnp.int32) + extra, rest)

    cos_b, sin_b = base(1.0 / 16.0, step)
    cos_a, sin_a = base(BASE / 16.0, jnp.zeros_like(step))
    unit = math.pi / (HIGH_END - LOW_END)
    rate = spread_ref[...] * (-0.5 * unit * unit * math.log2(math.e))
    out_ref[0, 0:BASE, :] = cos_a * 0.25
    out_ref[0, BASE : 2 * BASE, :] = sin_a * 0.25
    out_ref[0, 2 * BASE : 3 * BASE, :] = cos_b
    out_ref[0, 3 * BASE : 4 * BASE, :] = sin_b
    out_ref[0, 4 * BASE :, :] = jnp.broadcast_to(rate, (8, TABLE))

    @pl.when(pl.program_id(0) < READY)
    def _():
        table(out_ref.at[0], hi_ref.at[0], low_ref.at[0])


def choice_kernel(own_ref, out_ref):
    square = (LANES, LANES)
    down, across = iota(square, 0), iota(square, 1)
    names = jnp.concatenate(
        [own_ref[...].astype(F32), jnp.zeros((LANES - SCEN, LANES), F32)], axis=0
    ).T
    lower = (across < down).astype(F32).astype(BF16)
    owner = across.astype(F32)
    for s in range(SCEN):
        same = names[:, s : s + 1] == owner
        before = mm(lower, same.astype(F32).astype(BF16))
        for rank in range(MOST):
            out_ref[s, :, rank * LANES : (rank + 1) * LANES] = jnp.where(
                same & (before == float(rank)), 1.0, 0.0
            ).astype(BF16)


def table(base_ref, hi_ref, low_ref):
    step = iota((BASE, LANES), 0)
    stepf = step.astype(F32)
    for half in range(TABLE // LANES):
        at = slice(half * LANES, (half + 1) * LANES)
        cos_b = base_ref[2 * BASE : 3 * BASE, at]
        sin_b = base_ref[3 * BASE : 4 * BASE, at]
        rate = base_ref[4 * BASE : 4 * BASE + 1, at]
        for a in range(BASE):
            k = stepf + float(BASE * a)
            value = (
                base_ref[a : a + 1, at] * cos_b
                - base_ref[BASE + a : BASE + a + 1, at] * sin_b
            ) * jnp.exp2((k * k) * rate)
            if a == 0:
                value = jnp.where(step == 0, value * 0.5, value)
            hi = value.astype(BF16)
            hi_ref[a * BASE : (a + 1) * BASE, at] = hi
            low_ref[a * BASE : (a + 1) * BASE, at] = (value - hi.astype(F32)).astype(BF16)


def value_kernel(
    in_hbm, base_hbm, hi_hbm, low_hbm, out_hbm, mass_ref,
    in_ref, base_ref, hi_0, low_0, hi_1, low_1, hi_made, low_made, coef, values, grad, out_ref, sems, out_sems,
):
    width = 2 * LANES
    rows = MOST * LANES
    firsts = [
        pltpu.make_async_copy(base_hbm.at[READY], base_ref.at[0], sems.at[2, 0]),
        pltpu.make_async_copy(in_hbm, in_ref, sems.at[2, 1]),
        pltpu.make_async_copy(base_hbm.at[READY + 1], base_ref.at[1], sems.at[3, 0]),
    ]
    for copy in firsts:
        copy.start()
    copies = [
        (
            pltpu.make_async_copy(hi_hbm.at[block], hi_made.at[block], sems.at[0, block]),
            pltpu.make_async_copy(low_hbm.at[block], low_made.at[block], sems.at[1, block]),
        )
        for block in range(READY)
    ]
    for pair in copies:
        for copy in pair:
            copy.start()
    firsts[0].wait()
    table(base_ref.at[0], hi_0, low_0)
    firsts[1].wait()
    for rank in range(MOST):
        for chunk in range(CHUNKS):
            part = in_ref[pl.ds(rank * CHUNKS + chunk, DEVICES, stride=MSG1), :]
            hi = part.astype(BF16)
            at = slice(chunk * LANES, (chunk + 1) * LANES)
            coef[rank * LANES : (rank + 1) * LANES, at] = hi
            coef[rows + rank * LANES : rows + (rank + 1) * LANES, at] = (
                part - hi.astype(F32)
            ).astype(BF16)
    grad[...] = jnp.zeros_like(grad)
    firsts[2].wait()

    def multiply(block, hi_ref, low_ref):
        both = mm(coef[...], hi_ref[...])
        wide = both[:rows] + both[rows:] + mm(coef[:rows, :], low_ref[...])
        total = grad[...]
        for part in range(TABLE // width):
            s = block * (TABLE // width) + part
            tile = wide[:, part * width : (part + 1) * width]
            values[s] = tile
            for half in range(2):
                weights = in_ref[pl.ds((half * SCEN + s) * MSG1 + DUAL, 1), :]
                total = total + tile[:, half * LANES : (half + 1) * LANES] * weights
            start = s * OPT * MSG2
            for o in range(OPT):
                for rank in range(MOST):
                    for half in range(2):
                        out_ref[
                            pl.ds(start + o * MSG2 + (rank * 2 + half) * 8, 8), :
                        ] = tile[
                            rank * LANES + o * 8 : rank * LANES + o * 8 + 8,
                            half * LANES : (half + 1) * LANES,
                        ]
        grad[...] = total

    tiles = out_ref.reshape(DEVICES // 4, 17, 8, LANES)
    outs = []

    def send(*view):
        outs.append(
            pltpu.make_async_copy(tiles.at[view], out_hbm.at[view], out_sems.at[len(outs)])
        )
        outs[-1].start()

    def send_values(block):
        share = DEVICES // 4 // BLOCKS
        for first, last in ((0, 4), (5, 8), (9, 12), (13, 16)):
            send(slice(block * share, (block + 1) * share), slice(first, last))

    multiply(READY, hi_0, low_0)
    send_values(READY)
    table(base_ref.at[1], hi_1, low_1)
    multiply(READY + 1, hi_1, low_1)
    send_values(READY + 1)
    for block in range(READY):
        for copy in copies[block]:
            copy.wait()
        multiply(block, hi_made.at[block], low_made.at[block])
        send_values(block)

    mass = jnp.zeros((1, LANES), F32)
    for place in range(2 * SCEN):
        at = place * MSG1 + DUAL
        mass = mass + in_ref[at : at + 1, :]
    mass_ref[0] = jnp.sum(mass)
    extra = in_ref[pl.ds(PAIR, DEVICES, stride=MSG1), :]
    bars = []
    for rank in range(MOST):
        cost, pos = extra[:, 2 * rank : 2 * rank + 1], extra[:, 2 * rank + 1 : 2 * rank + 2]
        gradient = jnp.sum(
            grad[rank * LANES : (rank + 1) * LANES, :], axis=1, keepdims=True
        )
        bars.append(2.0 * primal(pos, cost, gradient) - pos)
    bar = jnp.broadcast_to(jnp.concatenate(bars, axis=0), (rows, LANES))
    for s in range(SCEN):
        for half in range(2):
            pnl = values[s, :, half * LANES : (half + 1) * LANES] * bar
            out_ref[pl.ds(s * OPT * MSG2 + MSG2 - 2 + half, OPT, stride=MSG2), :] = (
                jnp.broadcast_to(jnp.sum(pnl, axis=0, keepdims=True), (OPT, LANES))
            )
    for tile in (4, 8, 12, 16):
        send(slice(0, DEVICES // 4), slice(tile, tile + 1))
    for out in outs:
        out.wait()


def tile_kernel(
    in_ref, choice_ref, dual_ref, base_ref, mass_ref, level_ref,
    tile_ref, pay_ref, dual_out, tile_hbm, sems,
):
    level = level_ref[0]
    level_bar = 2.0 * level_step(level, mass_ref[0]) - level
    weights = []
    for half in range(2):
        pnl = jnp.sum(
            in_ref[pl.ds(MSG2 - 2 + half, DEVICES, stride=MSG2), :], axis=0, keepdims=True
        )
        weights.append(
            dual(dual_ref[half : half + 1, :], base_ref[half : half + 1, :], pnl, level_bar)
        )
        dual_out[half : half + 1, :] = weights[half]
    new = jnp.concatenate(weights, axis=1)
    old = jnp.concatenate([dual_ref[0:1, :], dual_ref[1:2, :]], axis=1)
    tall = iota((8, 2 * LANES), 0)
    both = jnp.where(
        tall == 0,
        jnp.broadcast_to(old, (8, 2 * LANES)),
        jnp.where(tall == 1, jnp.broadcast_to(new, (8, 2 * LANES)), 0.0),
    )
    rows, copies = [], []
    for s in range(SCEN):
        arrived = jnp.concatenate(
            [
                jnp.concatenate(
                    [
                        in_ref[pl.ds((rank * 2 + half) * 8 + s, DEVICES, stride=MSG2), :]
                        for half in range(2)
                    ],
                    axis=1,
                )
                for rank in range(MOST)
            ],
            axis=0,
        )
        tile = pick(choice_ref[s], arrived)
        at = slice(s * LANES, (s + 1) * LANES)
        tile_ref[at, :] = tile
        if s < STORED:
            copies.append(pltpu.make_async_copy(tile_ref.at[at], tile_hbm.at[at], sems.at[s]))
            copies[s].start()
        rows.append(
            lax.dot_general(both, tile, NT, precision=HIGHEST, preferred_element_type=F32)
        )
    payload = jnp.concatenate(
        [r[0:1, :] for r in rows]
        + [r[1:2, :] for r in rows]
        + [weights[0] + weights[1], jnp.zeros((PAYLOAD - 17, LANES), F32)],
        axis=0,
    )
    for s in range(SCEN):
        pay_ref[s * PAYLOAD : (s + 1) * PAYLOAD, :] = payload
    for copy in copies:
        copy.wait()


def position_kernel(
    in_ref, tile_ref, cost_ref, pos_ref, kept_ref, mass_ref, level_ref,
    pos_out, pnl_out, tile_hbm, level_out, bar_out, sem,
):
    rest = slice(STORED * LANES, SCEN * LANES)
    keep = pltpu.make_async_copy(tile_ref.at[rest], tile_hbm.at[rest], sem)
    keep.start()
    total = in_ref[0:PAYLOAD, :]
    for s in range(1, SCEN):
        total = total + in_ref[s * PAYLOAD : (s + 1) * PAYLOAD, :]
    level = level_step(level_ref[0], mass_ref[0])
    later = level_step(level, jnp.sum(total[16:17, :]))
    level_out[0] = later
    bar_out[0] = 2.0 * later - level
    cost = cost_ref[...]
    first = primal(pos_ref[...], cost, total[0:8, :])
    second = primal(first, cost, total[8:16, :])
    pos_out[...] = second
    bar = 2.0 * second - first
    pnl = jnp.zeros((8, 2 * LANES), F32)
    odd = (iota((8, LANES), 0) & 1) == 1
    for s in range(SCEN):
        line = jnp.broadcast_to(bar[s : s + 1, :], (8, LANES))
        upper = line.astype(BF16).astype(F32)
        parts = jnp.where(odd, line - upper, upper).astype(BF16)
        hi, low = two(tile_ref[s * LANES : (s + 1) * LANES, :])
        pnl = pnl + mm(parts, hi) + mm(parts, low)
    pnl = pnl[0:1, :] + pnl[1:2, :]
    for o in range(OPT):
        for half in range(2):
            pnl_out[o * 2 + half : o * 2 + half + 1, :] = pnl[:, half * LANES : (half + 1) * LANES]
    keep.wait()


VMEM = pl.BlockSpec(memory_space=pltpu.VMEM)
HBM = pl.BlockSpec(memory_space=pltpu.HBM)
SMEM = pl.BlockSpec(memory_space=pltpu.SMEM)


def exchange(x, axes):
    return lax.all_to_all(x, axes, split_axis=0, concat_axis=0, tiled=True)


def shaped(*shape, dtype=F32):
    return jax.ShapeDtypeStruct(shape, dtype)


def value_scratch():
    return [
        pltpu.VMEM((DEVICES * MSG1, LANES), F32),
        pltpu.VMEM((BLOCKS - READY, BASE_ROWS, TABLE), F32),
        *[pltpu.VMEM((TERMS, TABLE), BF16)] * 4,
        *[pltpu.VMEM((READY, TERMS, TABLE), BF16)] * 2,
        pltpu.VMEM((2 * MOST * LANES, TERMS), BF16),
        pltpu.VMEM((SCEN, MOST * LANES, 2 * LANES), F32),
        pltpu.VMEM((MOST * LANES, LANES), F32),
        pltpu.VMEM((DEVICES * MSG2, LANES), F32),
        pltpu.SemaphoreType.DMA((4, 2)),
        pltpu.SemaphoreType.DMA((4 * BLOCKS + 4,)),
    ]


def on_device(
    option_coefs,
    underlying_of,
    log_return_mean,
    log_return_spread,
    cost,
    positions,
    base_loss,
    duals,
    threshold,
):
    own = underlying_of.reshape(SCEN, LANES)
    cost = cost.reshape(SCEN, LANES)
    positions = positions.reshape(SCEN, LANES)
    base_loss = base_loss.reshape(2, LANES)
    duals = duals.reshape(2, LANES)

    sent = pl.pallas_call(
        send_kernel,
        out_shape=shaped(DEVICES * MSG1, LANES),
        in_specs=[HBM] * 5,
        out_specs=HBM,
        scratch_shapes=[
            pltpu.VMEM((SCEN, LANES), jnp.int32),
            pltpu.VMEM((LANES, TERMS), F32),
            pltpu.VMEM((SCEN, LANES), F32),
            pltpu.VMEM((SCEN, LANES), F32),
            pltpu.VMEM((2, LANES), F32),
            pltpu.VMEM((DEVICES * MSG1, LANES), F32),
            pltpu.SemaphoreType.DMA((5,)),
            pltpu.SemaphoreType.DMA((PARTS,)),
        ],
        compiler_params=params(63),
    )(own, option_coefs, cost, positions, duals)
    got = exchange(sent.reshape(DEVICES, MSG1 // 2, 2, LANES), OPT_AXES + SCEN_AXES)
    got = got.reshape(DEVICES * MSG1, LANES)

    made = pl.BlockSpec((1, TERMS, TABLE), lambda i: (jnp.minimum(i, READY - 1), 0, 0))
    base, made_hi, made_low = pl.pallas_call(
        base_kernel,
        grid=(BLOCKS,),
        out_shape=[
            pltpu.HBM((BLOCKS, BASE_ROWS, TABLE), F32),
            *[pltpu.HBM((READY, TERMS, TABLE), BF16)] * 2,
        ],
        in_specs=[pl.BlockSpec((1, TABLE), lambda i: (0, i))] * 2,
        out_specs=[pl.BlockSpec((1, BASE_ROWS, TABLE), lambda i: (i, 0, 0)), made, made],
        compiler_params=params(12),
        cost_estimate=pl.CostEstimate(
            flops=2 * TERMS * SCENARIOS,
            bytes_accessed=TERMS * SCENARIOS,
            transcendentals=0,
        ),
    )(log_return_mean, log_return_spread)
    choice = pl.pallas_call(
        choice_kernel,
        out_shape=shaped(SCEN, LANES, MOST * LANES, dtype=BF16),
        in_specs=[VMEM],
        out_specs=VMEM,
        compiler_params=params(4),
        cost_estimate=pl.CostEstimate(
            flops=TERMS * SCENARIOS, bytes_accessed=SCENARIOS, transcendentals=0
        ),
    )(own)

    values, mass = pl.pallas_call(
        value_kernel,
        out_shape=[shaped(DEVICES // 4, 17, 8, LANES), shaped(1)],
        in_specs=[HBM] * 4,
        out_specs=[HBM, SMEM],
        scratch_shapes=value_scratch(),
        compiler_params=params(63),
    )(got, base, made_hi, made_low)
    arrived = exchange(values.reshape(DEVICES, MSG2 // 2, 2, LANES), AXES)
    arrived = arrived.reshape(DEVICES * MSG2, LANES)

    tile, payload, first_duals, kept = pl.pallas_call(
        tile_kernel,
        out_shape=[
            shaped(SCEN * LANES, 2 * LANES),
            shaped(SCEN * PAYLOAD, LANES),
            shaped(2, LANES),
            shaped(SCEN * LANES, 2 * LANES),
        ],
        in_specs=[VMEM] * 4 + [SMEM] * 2,
        out_specs=[VMEM] * 3 + [HBM],
        scratch_shapes=[pltpu.SemaphoreType.DMA((STORED,))],
        compiler_params=params(12),
    )(arrived, choice, duals, base_loss, mass, threshold)
    gathered = exchange(payload.reshape(SCEN, PAYLOAD, LANES), SCEN_AXES[::-1])

    new_positions, part_pnl, kept, level, level_bar = pl.pallas_call(
        position_kernel,
        out_shape=[
            shaped(SCEN, LANES),
            shaped(OPT * 2, LANES),
            shaped(SCEN * LANES, 2 * LANES),
            shaped(1),
            shaped(1),
        ],
        in_specs=[VMEM] * 4 + [HBM] + [SMEM] * 2,
        out_specs=[VMEM] * 2 + [HBM] + [SMEM] * 2,
        input_output_aliases={4: 2},
        scratch_shapes=[pltpu.SemaphoreType.DMA(())],
        compiler_params=params(8),
    )(gathered.reshape(SCEN * PAYLOAD, LANES), tile, cost, positions, kept, mass, threshold)
    pnl = exchange(part_pnl.reshape(OPT, 2, LANES), OPT_AXES[::-1])

    new_duals = dual(first_duals, base_loss, jnp.sum(pnl, axis=0), level_bar)
    return (kept, new_positions.reshape(-1), new_duals.reshape(-1), level)


def solution(mesh):
    mesh = jax.sharding.Mesh(mesh.devices.reshape(SIZES), AXES)
    scen, opt = SCEN_AXES, OPT_AXES
    in_specs = (
        P(opt + scen, None),
        P(opt, None),
        P(AXES, None),
        P(AXES, None),
        P(opt),
        P(opt),
        P(scen),
        P(scen),
        P(),
    )
    out_specs = (P(opt, scen), P(opt), P(scen), P())
    return jax.shard_map(
        on_device, mesh=mesh, in_specs=in_specs, out_specs=out_specs, check_vma=False
    )
```

```python
import math

import jax
import jax.numpy as jnp
from jax import lax
from jax.experimental import pallas as pl
from jax.experimental.pallas import tpu as pltpu
from jax.sharding import PartitionSpec as P

LOW_END = -4.0
HIGH_END = 4.0
TAIL_LEVEL = 0.9
PRIMAL_STEP = 0.5
THRESH_STEP = 0.05
DUAL_STEP = 0.5

LANES = 128
SCEN = 8
OPT = 16
DEVICES = SCEN * OPT
TERMS = 1024
SCENARIOS = 2048
OPTIONS = 16384
MOST = 2
CHUNKS = TERMS // LANES
BASE = 32
TABLE = 512
BLOCKS = SCENARIOS // TABLE
READY = 3
BASE_ROWS = 4 * BASE + 8
PAIR = MOST * CHUNKS
DUAL = PAIR + 1
MSG1 = PAIR + 2
MSG2 = MOST * 16 + 2
PAYLOAD = 24
PARTS = 4
OUT_TILES = (2, 2, 4, 2, 17, 8, LANES)
STORED = 5
AXES = ("z_lo", "x", "z_hi", "y", "core")
SIZES = (2, 4, 2, 4, 2)
SCEN_AXES, OPT_AXES = AXES[:2], AXES[2:]
PLACES = ("z_hi", "z_lo", "y", "x", "core")
F32 = jnp.float32
BF16 = jnp.bfloat16
HIGHEST = lax.Precision.HIGHEST
NN = (((1,), (0,)), ((), ()))
NT = (((1,), (1,)), ((), ()))


def params(mib):
    return pltpu.CompilerParams(vmem_limit_bytes=int(mib * 1024 * 1024))


def iota(shape, axis):
    return lax.broadcasted_iota(jnp.int32, shape, axis)


def owner_of(place):
    return (place & (SCEN - 1)) * OPT + (place >> 3)


def place_of(scen, opt):
    (z_lo, x), (z_hi, rest) = divmod(scen, 4), divmod(opt, 8)
    y, core = divmod(rest, 2)
    return (((z_hi * 2 + z_lo) * 4 + y) * 4 + x) * 2 + core


def underlying_at(place):
    z_hi, z_lo, y, x = place >> 6, (place >> 5) & 1, (place >> 3) & 3, (place >> 1) & 3
    return (z_lo * 4 + x) * OPT + z_hi * 8 + y * 2 + (place & 1)


def mm(a, b, dims=NN):
    return lax.dot_general(a, b, dims, preferred_element_type=F32)


def three(x):
    hi = x.astype(BF16)
    rest = x - hi.astype(F32)
    mid = rest.astype(BF16)
    low = (rest - mid.astype(F32)).astype(BF16)
    return hi, mid, low


def two(x):
    hi = x.astype(BF16)
    return hi, (x - hi.astype(F32)).astype(BF16)


def pick(onehot, x, dims=NN):
    hi, mid, low = three(x)
    return mm(onehot, hi, dims) + mm(onehot, mid, dims) + mm(onehot, low, dims)


def level_step(level, mass):
    return level - THRESH_STEP * (1.0 - mass / ((1.0 - TAIL_LEVEL) * SCENARIOS))


def primal(position, cost, gradient):
    return jnp.clip(
        position - PRIMAL_STEP * (cost - gradient / math.sqrt(SCENARIOS)), -1.0, 1.0
    )


def dual(weights, base, pnl, level_bar):
    return jnp.clip(
        weights + DUAL_STEP * (base - pnl / math.sqrt(OPTIONS) - level_bar), 0.0, 1.0
    )


def send_kernel(
    own_hbm, coef_hbm, cost_hbm, pos_hbm, dual_hbm, out_hbm,
    own_ref, coef_ref, cost_ref, pos_ref, dual_ref, out_ref, sems, out_sems,
):
    pairs = (
        (own_hbm, own_ref),
        (cost_hbm, cost_ref),
        (pos_hbm, pos_ref),
        (dual_hbm, dual_ref),
        (coef_hbm, coef_ref),
    )
    copies = [pltpu.make_async_copy(a, b, sems.at[i]) for i, (a, b) in enumerate(pairs)]
    for copy in copies:
        copy.start()
    for copy in copies[:4]:
        copy.wait()
    row = lax.axis_index("z_lo") * 4 + lax.axis_index("x")
    half = lax.axis_index("core")
    square = (LANES, LANES)
    down, across = iota(square, 0), iota(square, 1)
    same = own_ref[pl.ds(row, 1), :] == owner_of(down)
    before = mm(
        same.astype(F32).astype(BF16), (down < across).astype(F32).astype(BF16)
    )
    cost = jnp.broadcast_to(cost_ref[pl.ds(row, 1), :], square)
    pos = jnp.broadcast_to(pos_ref[pl.ds(row, 1), :], square)
    chosen = [
        jnp.where(same & (before == float(rank)), 1.0, 0.0).astype(BF16)
        for rank in range(MOST)
    ]
    pair = jnp.zeros(square, F32)
    for rank in range(MOST):
        packed = jnp.where(
            down == 2 * rank, cost, jnp.where(down == 2 * rank + 1, pos, 0.0)
        )
        pair = pair + pick(chosen[rank], packed, NT)
    out_ref[pl.ds(PAIR, DEVICES, stride=MSG1), :] = pair
    out_ref[pl.ds(DUAL, DEVICES, stride=MSG1), :] = jnp.broadcast_to(
        dual_ref[pl.ds(half, 1), :], square
    )
    copies[4].wait()
    hi, mid = two(coef_ref[...])
    size = DEVICES // PARTS
    outs = []
    for part in range(PARTS):
        for rank in range(MOST):
            some = chosen[rank][part * size : (part + 1) * size, :]
            rows = mm(some, hi) + mm(some, mid)
            for chunk in range(CHUNKS):
                start = part * size * MSG1 + rank * CHUNKS + chunk
                out_ref[pl.ds(start, size, stride=MSG1), :] = rows[
                    :, chunk * LANES : (chunk + 1) * LANES
                ]
        at = slice(part * size * MSG1, (part + 1) * size * MSG1)
        outs.append(
            pltpu.make_async_copy(out_ref.at[at], out_hbm.at[at], out_sems.at[part])
        )
        outs[part].start()
    for out in outs:
        out.wait()


def turn(quarters, rest):
    x = rest * (2.0 * math.pi)
    z = x * x
    sin = x * (
        1.0 + z * (-1 / 6 + z * (1 / 120 + z * (-1 / 5040 + z * (1 / 362880))))
    )
    cos = 1.0 + z * (
        -1 / 2 + z * (1 / 24 + z * (-1 / 720 + z * (1 / 40320 - z * (1 / 3628800))))
    )
    swap = (quarters & 1) == 1
    cos_out = jnp.where(swap, sin, cos)
    sin_out = jnp.where(swap, cos, sin)
    cos_out = jnp.where(((quarters + 1) & 2) == 2, -cos_out, cos_out)
    sin_out = jnp.where((quarters & 2) == 2, -sin_out, sin_out)
    return cos_out, sin_out


def base_kernel(mean_ref, spread_ref, out_ref, hi_ref, low_ref):
    shape = (BASE, TABLE)
    mean = mean_ref[...]
    coarse = jnp.round(mean * 2048.0) * (1.0 / 2048.0)
    fine = mean - coarse
    step = iota(shape, 0)
    stepf = step.astype(F32)

    def base(scale, extra):
        turns = (stepf * scale) * coarse
        quarters = jnp.round(turns * 4.0)
        rest = (turns - quarters * 0.25) + (stepf * scale) * fine
        return turn(quarters.astype(jnp.int32) + extra, rest)

    cos_b, sin_b = base(1.0 / 16.0, step)
    cos_a, sin_a = base(BASE / 16.0, jnp.zeros_like(step))
    unit = math.pi / (HIGH_END - LOW_END)
    rate = spread_ref[...] * (-0.5 * unit * unit * math.log2(math.e))
    out_ref[0, 0:BASE, :] = cos_a * 0.25
    out_ref[0, BASE : 2 * BASE, :] = sin_a * 0.25
    out_ref[0, 2 * BASE : 3 * BASE, :] = cos_b
    out_ref[0, 3 * BASE : 4 * BASE, :] = sin_b
    out_ref[0, 4 * BASE :, :] = jnp.broadcast_to(rate, (8, TABLE))

    @pl.when(pl.program_id(0) < READY)
    def _():
        table(out_ref.at[0], hi_ref.at[0], low_ref.at[0])


def choice_kernel(own_ref, out_ref):
    square = (LANES, LANES)
    down, across = iota(square, 0), iota(square, 1)
    names = jnp.concatenate(
        [own_ref[...].astype(F32), jnp.zeros((LANES - SCEN, LANES), F32)], axis=0
    ).T
    lower = (across < down).astype(F32).astype(BF16)
    owner = underlying_at(across).astype(F32)
    for s in range(SCEN):
        same = names[:, s : s + 1] == owner
        before = mm(lower, same.astype(F32).astype(BF16))
        for rank in range(MOST):
            out_ref[s, :, rank * LANES : (rank + 1) * LANES] = jnp.where(
                same & (before == float(rank)), 1.0, 0.0
            ).astype(BF16)


def table(base_ref, hi_ref, low_ref):
    step = iota((BASE, LANES), 0)
    stepf = step.astype(F32)
    for half in range(TABLE // LANES):
        at = slice(half * LANES, (half + 1) * LANES)
        cos_b = base_ref[2 * BASE : 3 * BASE, at]
        sin_b = base_ref[3 * BASE : 4 * BASE, at]
        rate = base_ref[4 * BASE : 4 * BASE + 1, at]
        for a in range(BASE):
            k = stepf + float(BASE * a)
            value = (
                base_ref[a : a + 1, at] * cos_b
                - base_ref[BASE + a : BASE + a + 1, at] * sin_b
            ) * jnp.exp2((k * k) * rate)
            if a == 0:
                value = jnp.where(step == 0, value * 0.5, value)
            hi = value.astype(BF16)
            hi_ref[a * BASE : (a + 1) * BASE, at] = hi
            low_ref[a * BASE : (a + 1) * BASE, at] = (value - hi.astype(F32)).astype(BF16)


def value_kernel(
    in_hbm, base_hbm, hi_hbm, low_hbm, out_hbm, mass_ref,
    in_ref, base_ref, hi_0, low_0, hi_made, low_made, coef, values, grad, out_ref, sems, out_sems,
):
    width = 2 * LANES
    rows = MOST * LANES
    firsts = [
        pltpu.make_async_copy(base_hbm.at[READY], base_ref.at[0], sems.at[2, 0]),
        pltpu.make_async_copy(in_hbm, in_ref, sems.at[2, 1]),
    ]
    for copy in firsts:
        copy.start()
    copies = [
        (
            pltpu.make_async_copy(hi_hbm.at[block], hi_made.at[block], sems.at[0, block]),
            pltpu.make_async_copy(low_hbm.at[block], low_made.at[block], sems.at[1, block]),
        )
        for block in range(READY)
    ]
    for pair in copies:
        for copy in pair:
            copy.start()
    firsts[0].wait()
    table(base_ref.at[0], hi_0, low_0)
    firsts[1].wait()
    for rank in range(MOST):
        for chunk in range(CHUNKS):
            part = in_ref[pl.ds(rank * CHUNKS + chunk, DEVICES, stride=MSG1), :]
            hi = part.astype(BF16)
            at = slice(chunk * LANES, (chunk + 1) * LANES)
            coef[rank * LANES : (rank + 1) * LANES, at] = hi
            coef[rows + rank * LANES : rows + (rank + 1) * LANES, at] = (
                part - hi.astype(F32)
            ).astype(BF16)
    grad[...] = jnp.zeros_like(grad)

    def multiply(block, hi_ref, low_ref):
        both = mm(coef[...], hi_ref[...])
        wide = both[:rows] + both[rows:] + mm(coef[:rows, :], low_ref[...])
        total = grad[...]
        for part in range(TABLE // width):
            s = block * (TABLE // width) + part
            tile = wide[:, part * width : (part + 1) * width]
            values[s] = tile
            for half in range(2):
                weights = in_ref[pl.ds((half * SCEN + s) * MSG1 + DUAL, 1), :]
                total = total + tile[:, half * LANES : (half + 1) * LANES] * weights
            for o in range(OPT):
                start = place_of(s, o) * MSG2
                for rank in range(MOST):
                    for half in range(2):
                        out_ref[
                            pl.ds(start + (rank * 2 + half) * 8, 8), :
                        ] = tile[
                            rank * LANES + o * 8 : rank * LANES + o * 8 + 8,
                            half * LANES : (half + 1) * LANES,
                        ]
        grad[...] = total

    tiles = out_ref.reshape(OUT_TILES)
    outs = []

    def send(*view):
        outs.append(
            pltpu.make_async_copy(tiles.at[view], out_hbm.at[view], out_sems.at[len(outs)])
        )
        outs[-1].start()

    def send_values(block):
        every, (z_lo, x_pair) = slice(None), divmod(block, 2)
        for first, last in ((0, 4), (5, 8), (9, 12), (13, 16)):
            send(every, z_lo, every, x_pair, slice(first, last))

    multiply(READY, hi_0, low_0)
    send_values(READY)
    for block in range(READY):
        for copy in copies[block]:
            copy.wait()
        multiply(block, hi_made.at[block], low_made.at[block])
        send_values(block)

    mass = jnp.zeros((1, LANES), F32)
    for place in range(2 * SCEN):
        at = place * MSG1 + DUAL
        mass = mass + in_ref[at : at + 1, :]
    mass_ref[0] = jnp.sum(mass)
    extra = in_ref[pl.ds(PAIR, DEVICES, stride=MSG1), :]
    bars = []
    for rank in range(MOST):
        cost, pos = extra[:, 2 * rank : 2 * rank + 1], extra[:, 2 * rank + 1 : 2 * rank + 2]
        gradient = jnp.sum(
            grad[rank * LANES : (rank + 1) * LANES, :], axis=1, keepdims=True
        )
        bars.append(2.0 * primal(pos, cost, gradient) - pos)
    bar = jnp.broadcast_to(jnp.concatenate(bars, axis=0), (rows, LANES))
    for s in range(SCEN):
        for half in range(2):
            pnl = values[s, :, half * LANES : (half + 1) * LANES] * bar
            pnl = jnp.broadcast_to(jnp.sum(pnl, axis=0, keepdims=True), (4, LANES))
            for o in (0, 1, 8, 9):
                first = place_of(s, o) * MSG2 + MSG2 - 2 + half
                out_ref[pl.ds(first, 4, stride=8 * MSG2), :] = pnl
    for tile in (4, 8, 12, 16):
        send(*[slice(None)] * 4, slice(tile, tile + 1))
    for out in outs:
        out.wait()


def tile_kernel(
    in_ref, choice_ref, dual_ref, base_ref, mass_ref, level_ref,
    tile_ref, pay_ref, dual_out, tile_hbm, sems,
):
    level = level_ref[0]
    level_bar = 2.0 * level_step(level, mass_ref[0]) - level
    weights = []
    for half in range(2):
        pnl = jnp.sum(
            in_ref[pl.ds(MSG2 - 2 + half, DEVICES, stride=MSG2), :], axis=0, keepdims=True
        )
        weights.append(
            dual(dual_ref[half : half + 1, :], base_ref[half : half + 1, :], pnl, level_bar)
        )
        dual_out[half : half + 1, :] = weights[half]
    new = jnp.concatenate(weights, axis=1)
    old = jnp.concatenate([dual_ref[0:1, :], dual_ref[1:2, :]], axis=1)
    tall = iota((8, 2 * LANES), 0)
    both = jnp.where(
        tall == 0,
        jnp.broadcast_to(old, (8, 2 * LANES)),
        jnp.where(tall == 1, jnp.broadcast_to(new, (8, 2 * LANES)), 0.0),
    )
    rows, copies = [], []
    for s in range(SCEN):
        arrived = jnp.concatenate(
            [
                jnp.concatenate(
                    [
                        in_ref[pl.ds((rank * 2 + half) * 8 + s, DEVICES, stride=MSG2), :]
                        for half in range(2)
                    ],
                    axis=1,
                )
                for rank in range(MOST)
            ],
            axis=0,
        )
        tile = pick(choice_ref[s], arrived)
        at = slice(s * LANES, (s + 1) * LANES)
        tile_ref[at, :] = tile
        if s < STORED:
            copies.append(pltpu.make_async_copy(tile_ref.at[at], tile_hbm.at[at], sems.at[s]))
            copies[s].start()
        rows.append(
            lax.dot_general(both, tile, NT, precision=HIGHEST, preferred_element_type=F32)
        )
    payload = jnp.concatenate(
        [r[0:1, :] for r in rows]
        + [r[1:2, :] for r in rows]
        + [weights[0] + weights[1], jnp.zeros((PAYLOAD - 17, LANES), F32)],
        axis=0,
    )
    for s in range(SCEN):
        pay_ref[s * PAYLOAD : (s + 1) * PAYLOAD, :] = payload
    for copy in copies:
        copy.wait()


def position_kernel(
    in_ref, tile_ref, cost_ref, pos_ref, kept_ref, mass_ref, level_ref,
    pos_out, pnl_out, tile_hbm, level_out, bar_out, sem,
):
    rest = slice(STORED * LANES, SCEN * LANES)
    keep = pltpu.make_async_copy(tile_ref.at[rest], tile_hbm.at[rest], sem)
    keep.start()
    total = in_ref[0:PAYLOAD, :]
    for s in range(1, SCEN):
        total = total + in_ref[s * PAYLOAD : (s + 1) * PAYLOAD, :]
    level = level_step(level_ref[0], mass_ref[0])
    later = level_step(level, jnp.sum(total[16:17, :]))
    level_out[0] = later
    bar_out[0] = 2.0 * later - level
    cost = cost_ref[...]
    first = primal(pos_ref[...], cost, total[0:8, :])
    second = primal(first, cost, total[8:16, :])
    pos_out[...] = second
    bar = 2.0 * second - first
    pnl = jnp.zeros((8, 2 * LANES), F32)
    odd = (iota((8, LANES), 0) & 1) == 1
    for s in range(SCEN):
        line = jnp.broadcast_to(bar[s : s + 1, :], (8, LANES))
        upper = line.astype(BF16).astype(F32)
        parts = jnp.where(odd, line - upper, upper).astype(BF16)
        hi, low = two(tile_ref[s * LANES : (s + 1) * LANES, :])
        pnl = pnl + mm(parts, hi) + mm(parts, low)
    pnl = pnl[0:1, :] + pnl[1:2, :]
    for o in range(OPT):
        for half in range(2):
            pnl_out[o * 2 + half : o * 2 + half + 1, :] = pnl[:, half * LANES : (half + 1) * LANES]
    keep.wait()


VMEM = pl.BlockSpec(memory_space=pltpu.VMEM)
HBM = pl.BlockSpec(memory_space=pltpu.HBM)
SMEM = pl.BlockSpec(memory_space=pltpu.SMEM)


def exchange(x, axes):
    return lax.all_to_all(x, axes, split_axis=0, concat_axis=0, tiled=True)


def shaped(*shape, dtype=F32):
    return jax.ShapeDtypeStruct(shape, dtype)


def value_scratch():
    return [
        pltpu.VMEM((DEVICES * MSG1, LANES), F32),
        pltpu.VMEM((BLOCKS - READY, BASE_ROWS, TABLE), F32),
        *[pltpu.VMEM((TERMS, TABLE), BF16)] * 2,
        *[pltpu.VMEM((READY, TERMS, TABLE), BF16)] * 2,
        pltpu.VMEM((2 * MOST * LANES, TERMS), BF16),
        pltpu.VMEM((SCEN, MOST * LANES, 2 * LANES), F32),
        pltpu.VMEM((MOST * LANES, LANES), F32),
        pltpu.VMEM((DEVICES * MSG2, LANES), F32),
        pltpu.SemaphoreType.DMA((4, READY)),
        pltpu.SemaphoreType.DMA((4 * BLOCKS + 4,)),
    ]


def on_device(
    option_coefs,
    underlying_of,
    log_return_mean,
    log_return_spread,
    cost,
    positions,
    base_loss,
    duals,
    threshold,
):
    own = underlying_of.reshape(SCEN, LANES)
    cost = cost.reshape(SCEN, LANES)
    positions = positions.reshape(SCEN, LANES)
    base_loss = base_loss.reshape(2, LANES)
    duals = duals.reshape(2, LANES)

    sent = pl.pallas_call(
        send_kernel,
        out_shape=shaped(DEVICES * MSG1, LANES),
        in_specs=[HBM] * 5,
        out_specs=HBM,
        scratch_shapes=[
            pltpu.VMEM((SCEN, LANES), jnp.int32),
            pltpu.VMEM((LANES, TERMS), F32),
            pltpu.VMEM((SCEN, LANES), F32),
            pltpu.VMEM((SCEN, LANES), F32),
            pltpu.VMEM((2, LANES), F32),
            pltpu.VMEM((DEVICES * MSG1, LANES), F32),
            pltpu.SemaphoreType.DMA((5,)),
            pltpu.SemaphoreType.DMA((PARTS,)),
        ],
        compiler_params=params(63),
    )(own, option_coefs, cost, positions, duals)
    got = exchange(sent.reshape(DEVICES, MSG1 // 2, 2, LANES), OPT_AXES + SCEN_AXES)
    got = got.reshape(DEVICES * MSG1, LANES)

    made = pl.BlockSpec((1, TERMS, TABLE), lambda i: (jnp.minimum(i, READY - 1), 0, 0))
    base, made_hi, made_low = pl.pallas_call(
        base_kernel,
        grid=(BLOCKS,),
        out_shape=[
            pltpu.HBM((BLOCKS, BASE_ROWS, TABLE), F32),
            *[pltpu.HBM((READY, TERMS, TABLE), BF16)] * 2,
        ],
        in_specs=[pl.BlockSpec((1, TABLE), lambda i: (0, i))] * 2,
        out_specs=[pl.BlockSpec((1, BASE_ROWS, TABLE), lambda i: (i, 0, 0)), made, made],
        compiler_params=params(12),
        cost_estimate=pl.CostEstimate(
            flops=2 * TERMS * SCENARIOS,
            bytes_accessed=TERMS * SCENARIOS,
            transcendentals=0,
        ),
    )(log_return_mean, log_return_spread)
    choice = pl.pallas_call(
        choice_kernel,
        out_shape=shaped(SCEN, LANES, MOST * LANES, dtype=BF16),
        in_specs=[VMEM],
        out_specs=VMEM,
        compiler_params=params(4),
        cost_estimate=pl.CostEstimate(
            flops=TERMS * SCENARIOS, bytes_accessed=SCENARIOS, transcendentals=0
        ),
    )(own)

    values, mass = pl.pallas_call(
        value_kernel,
        out_shape=[shaped(*OUT_TILES), shaped(1)],
        in_specs=[HBM] * 4,
        out_specs=[HBM, SMEM],
        scratch_shapes=value_scratch(),
        compiler_params=params(63),
    )(got, base, made_hi, made_low)
    arrived = exchange(values.reshape(DEVICES, MSG2 // 2, 2, LANES), PLACES)
    arrived = arrived.reshape(DEVICES * MSG2, LANES)

    tile, payload, first_duals, kept = pl.pallas_call(
        tile_kernel,
        out_shape=[
            shaped(SCEN * LANES, 2 * LANES),
            shaped(SCEN * PAYLOAD, LANES),
            shaped(2, LANES),
            shaped(SCEN * LANES, 2 * LANES),
        ],
        in_specs=[VMEM] * 4 + [SMEM] * 2,
        out_specs=[VMEM] * 3 + [HBM],
        scratch_shapes=[pltpu.SemaphoreType.DMA((STORED,))],
        compiler_params=params(12),
    )(arrived, choice, duals, base_loss, mass, threshold)
    gathered = exchange(payload.reshape(SCEN, PAYLOAD, LANES), SCEN_AXES[::-1])

    new_positions, part_pnl, kept, level, level_bar = pl.pallas_call(
        position_kernel,
        out_shape=[
            shaped(SCEN, LANES),
            shaped(OPT * 2, LANES),
            shaped(SCEN * LANES, 2 * LANES),
            shaped(1),
            shaped(1),
        ],
        in_specs=[VMEM] * 4 + [HBM] + [SMEM] * 2,
        out_specs=[VMEM] * 2 + [HBM] + [SMEM] * 2,
        input_output_aliases={4: 2},
        scratch_shapes=[pltpu.SemaphoreType.DMA(())],
        compiler_params=params(8),
    )(gathered.reshape(SCEN * PAYLOAD, LANES), tile, cost, positions, kept, mass, threshold)
    pnl = exchange(part_pnl.reshape(OPT, 2, LANES), OPT_AXES[::-1])

    new_duals = dual(first_duals, base_loss, jnp.sum(pnl, axis=0), level_bar)
    return (kept, new_positions.reshape(-1), new_duals.reshape(-1), level)


def solution(mesh):
    mesh = jax.sharding.Mesh(mesh.devices.reshape(SIZES), AXES)
    scen, opt = SCEN_AXES, OPT_AXES
    in_specs = (
        P(opt + scen, None),
        P(opt, None),
        P(AXES, None),
        P(AXES, None),
        P(opt),
        P(opt),
        P(scen),
        P(scen),
        P(),
    )
    out_specs = (P(opt, scen), P(opt), P(scen), P())
    return jax.shard_map(
        on_device, mesh=mesh, in_specs=in_specs, out_specs=out_specs, check_vma=False
    )
```

```python
import math

import jax
import jax.numpy as jnp
from jax import lax
from jax.experimental import pallas as pl
from jax.experimental.pallas import tpu as pltpu
from jax.sharding import PartitionSpec as P

LOW_END = -4.0
HIGH_END = 4.0
TAIL_LEVEL = 0.9
PRIMAL_STEP = 0.5
THRESH_STEP = 0.05
DUAL_STEP = 0.5

LANES = 128
SCEN = 8
OPT = 16
DEVICES = SCEN * OPT
TERMS = 1024
SCENARIOS = 2048
OPTIONS = 16384
MOST = 2
CHUNKS = TERMS // LANES
BASE = 32
TABLE = 512
BLOCKS = SCENARIOS // TABLE
READY = 3
BASE_ROWS = 4 * BASE + 8
PAIR = MOST * CHUNKS
DUAL = PAIR + 1
MSG1 = PAIR + 2
MSG2 = MOST * 16 + 2
PAYLOAD = 24
PARTS = 4
OUT_TILES = (2, 2, 4, 2, 17, 8, LANES)
STORED = 5
AXES = ("z_lo", "x", "z_hi", "y", "core")
SIZES = (2, 4, 2, 4, 2)
SCEN_AXES, OPT_AXES = AXES[:2], AXES[2:]
PLACES = ("z_hi", "z_lo", "y", "x", "core")
F32 = jnp.float32
BF16 = jnp.bfloat16
HIGHEST = lax.Precision.HIGHEST
NN = (((1,), (0,)), ((), ()))
NT = (((1,), (1,)), ((), ()))


def params(mib):
    return pltpu.CompilerParams(vmem_limit_bytes=int(mib * 1024 * 1024))


def iota(shape, axis):
    return lax.broadcasted_iota(jnp.int32, shape, axis)


def owner_of(place):
    return (place & (SCEN - 1)) * OPT + (place >> 3)


def place_of(scen, opt):
    (z_lo, x), (z_hi, rest) = divmod(scen, 4), divmod(opt, 8)
    y, core = divmod(rest, 2)
    return (((z_hi * 2 + z_lo) * 4 + y) * 4 + x) * 2 + core


def underlying_at(place):
    z_hi, z_lo, y, x = place >> 6, (place >> 5) & 1, (place >> 3) & 3, (place >> 1) & 3
    return (z_lo * 4 + x) * OPT + z_hi * 8 + y * 2 + (place & 1)


def mm(a, b, dims=NN):
    return lax.dot_general(a, b, dims, preferred_element_type=F32)


def three(x):
    hi = x.astype(BF16)
    rest = x - hi.astype(F32)
    mid = rest.astype(BF16)
    low = (rest - mid.astype(F32)).astype(BF16)
    return hi, mid, low


def two(x):
    hi = x.astype(BF16)
    return hi, (x - hi.astype(F32)).astype(BF16)


def pick(onehot, x, dims=NN):
    hi, mid, low = three(x)
    return mm(onehot, hi, dims) + mm(onehot, mid, dims) + mm(onehot, low, dims)


def level_step(level, mass):
    return level - THRESH_STEP * (1.0 - mass / ((1.0 - TAIL_LEVEL) * SCENARIOS))


def primal(position, cost, gradient):
    return jnp.clip(
        position - PRIMAL_STEP * (cost - gradient / math.sqrt(SCENARIOS)), -1.0, 1.0
    )


def dual(weights, base, pnl, level_bar):
    return jnp.clip(
        weights + DUAL_STEP * (base - pnl / math.sqrt(OPTIONS) - level_bar), 0.0, 1.0
    )


def send_kernel(
    own_hbm, coef_hbm, cost_hbm, pos_hbm, dual_hbm, out_hbm,
    own_ref, coef_ref, cost_ref, pos_ref, dual_ref, out_ref, sems, out_sems,
):
    pairs = (
        (own_hbm, own_ref),
        (cost_hbm, cost_ref),
        (pos_hbm, pos_ref),
        (dual_hbm, dual_ref),
        (coef_hbm, coef_ref),
    )
    copies = [pltpu.make_async_copy(a, b, sems.at[i]) for i, (a, b) in enumerate(pairs)]
    for copy in copies:
        copy.start()
    for copy in copies[:4]:
        copy.wait()
    row = lax.axis_index("z_lo") * 4 + lax.axis_index("x")
    half = lax.axis_index("core")
    square = (LANES, LANES)
    down, across = iota(square, 0), iota(square, 1)
    same = own_ref[pl.ds(row, 1), :] == owner_of(down)
    before = mm(
        same.astype(F32).astype(BF16), (down < across).astype(F32).astype(BF16)
    )
    cost = jnp.broadcast_to(cost_ref[pl.ds(row, 1), :], square)
    pos = jnp.broadcast_to(pos_ref[pl.ds(row, 1), :], square)
    chosen = [
        jnp.where(same & (before == float(rank)), 1.0, 0.0).astype(BF16)
        for rank in range(MOST)
    ]
    pair = jnp.zeros(square, F32)
    for rank in range(MOST):
        packed = jnp.where(
            down == 2 * rank, cost, jnp.where(down == 2 * rank + 1, pos, 0.0)
        )
        pair = pair + pick(chosen[rank], packed, NT)
    out_ref[pl.ds(PAIR, DEVICES, stride=MSG1), :] = pair
    out_ref[pl.ds(DUAL, DEVICES, stride=MSG1), :] = jnp.broadcast_to(
        dual_ref[pl.ds(half, 1), :], square
    )
    copies[4].wait()
    hi, mid = two(coef_ref[...])
    size = DEVICES // PARTS
    outs = []
    for part in range(PARTS):
        for rank in range(MOST):
            some = chosen[rank][part * size : (part + 1) * size, :]
            rows = mm(some, hi) + mm(some, mid)
            for chunk in range(CHUNKS):
                start = part * size * MSG1 + rank * CHUNKS + chunk
                out_ref[pl.ds(start, size, stride=MSG1), :] = rows[
                    :, chunk * LANES : (chunk + 1) * LANES
                ]
        at = slice(part * size * MSG1, (part + 1) * size * MSG1)
        outs.append(
            pltpu.make_async_copy(out_ref.at[at], out_hbm.at[at], out_sems.at[part])
        )
        outs[part].start()
    for out in outs:
        out.wait()


def turn(quarters, rest):
    x = rest * (2.0 * math.pi)
    z = x * x
    sin = x * (
        1.0 + z * (-1 / 6 + z * (1 / 120 + z * (-1 / 5040 + z * (1 / 362880))))
    )
    cos = 1.0 + z * (
        -1 / 2 + z * (1 / 24 + z * (-1 / 720 + z * (1 / 40320 - z * (1 / 3628800))))
    )
    swap = (quarters & 1) == 1
    cos_out = jnp.where(swap, sin, cos)
    sin_out = jnp.where(swap, cos, sin)
    cos_out = jnp.where(((quarters + 1) & 2) == 2, -cos_out, cos_out)
    sin_out = jnp.where((quarters & 2) == 2, -sin_out, sin_out)
    return cos_out, sin_out


def base_kernel(mean_ref, spread_ref, out_ref, hi_ref, low_ref):
    shape = (BASE, TABLE)
    mean = mean_ref[...]
    coarse = jnp.round(mean * 2048.0) * (1.0 / 2048.0)
    fine = mean - coarse
    step = iota(shape, 0)
    stepf = step.astype(F32)

    def base(scale, extra):
        turns = (stepf * scale) * coarse
        quarters = jnp.round(turns * 4.0)
        rest = (turns - quarters * 0.25) + (stepf * scale) * fine
        return turn(quarters.astype(jnp.int32) + extra, rest)

    cos_b, sin_b = base(1.0 / 16.0, step)
    cos_a, sin_a = base(BASE / 16.0, jnp.zeros_like(step))
    unit = math.pi / (HIGH_END - LOW_END)
    rate = spread_ref[...] * (-0.5 * unit * unit * math.log2(math.e))
    out_ref[0, 0:BASE, :] = cos_a * 0.25
    out_ref[0, BASE : 2 * BASE, :] = sin_a * 0.25
    out_ref[0, 2 * BASE : 3 * BASE, :] = cos_b
    out_ref[0, 3 * BASE : 4 * BASE, :] = sin_b
    out_ref[0, 4 * BASE :, :] = jnp.broadcast_to(rate, (8, TABLE))

    @pl.when(pl.program_id(0) < READY)
    def _():
        table(out_ref.at[0], hi_ref.at[0], low_ref.at[0])


def choice_kernel(own_ref, in_hbm, out_ref, mass_ref, in_ref, sem):
    first = pltpu.make_async_copy(in_hbm.at[0 : 2 * SCEN * MSG1], in_ref, sem)
    first.start()
    square = (LANES, LANES)
    down, across = iota(square, 0), iota(square, 1)
    names = jnp.concatenate(
        [own_ref[...].astype(F32), jnp.zeros((LANES - SCEN, LANES), F32)], axis=0
    ).T
    lower = (across < down).astype(F32).astype(BF16)
    owner = underlying_at(across).astype(F32)
    for s in range(SCEN):
        same = names[:, s : s + 1] == owner
        before = mm(lower, same.astype(F32).astype(BF16))
        for rank in range(MOST):
            out_ref[s, :, rank * LANES : (rank + 1) * LANES] = jnp.where(
                same & (before == float(rank)), 1.0, 0.0
            ).astype(BF16)
    first.wait()
    mass = jnp.zeros((1, LANES), F32)
    for place in range(2 * SCEN):
        at = place * MSG1 + DUAL
        mass = mass + in_ref[at : at + 1, :]
    mass_ref[0] = jnp.sum(mass)


def table(base_ref, hi_ref, low_ref):
    step = iota((BASE, LANES), 0)
    stepf = step.astype(F32)
    for half in range(TABLE // LANES):
        at = slice(half * LANES, (half + 1) * LANES)
        cos_b = base_ref[2 * BASE : 3 * BASE, at]
        sin_b = base_ref[3 * BASE : 4 * BASE, at]
        rate = base_ref[4 * BASE : 4 * BASE + 1, at]
        for a in range(BASE):
            k = stepf + float(BASE * a)
            value = (
                base_ref[a : a + 1, at] * cos_b
                - base_ref[BASE + a : BASE + a + 1, at] * sin_b
            ) * jnp.exp2((k * k) * rate)
            if a == 0:
                value = jnp.where(step == 0, value * 0.5, value)
            hi = value.astype(BF16)
            hi_ref[a * BASE : (a + 1) * BASE, at] = hi
            low_ref[a * BASE : (a + 1) * BASE, at] = (value - hi.astype(F32)).astype(BF16)


def value_kernel(
    in_hbm, base_hbm, hi_hbm, low_hbm, out_hbm,
    in_ref, base_ref, hi_0, low_0, hi_made, low_made, coef, values, grad, out_ref, sems, out_sems,
):
    width = 2 * LANES
    rows = MOST * LANES
    firsts = [
        pltpu.make_async_copy(base_hbm.at[READY], base_ref.at[0], sems.at[2, 0]),
        pltpu.make_async_copy(in_hbm, in_ref, sems.at[2, 1]),
    ]
    for copy in firsts:
        copy.start()
    copies = [
        (
            pltpu.make_async_copy(hi_hbm.at[block], hi_made.at[block], sems.at[0, block]),
            pltpu.make_async_copy(low_hbm.at[block], low_made.at[block], sems.at[1, block]),
        )
        for block in range(READY)
    ]
    for pair in copies:
        for copy in pair:
            copy.start()
    firsts[0].wait()
    table(base_ref.at[0], hi_0, low_0)
    firsts[1].wait()
    for rank in range(MOST):
        for chunk in range(CHUNKS):
            part = in_ref[pl.ds(rank * CHUNKS + chunk, DEVICES, stride=MSG1), :]
            hi = part.astype(BF16)
            at = slice(chunk * LANES, (chunk + 1) * LANES)
            coef[rank * LANES : (rank + 1) * LANES, at] = hi
            coef[rows + rank * LANES : rows + (rank + 1) * LANES, at] = (
                part - hi.astype(F32)
            ).astype(BF16)
    grad[...] = jnp.zeros_like(grad)

    def multiply(block, hi_ref, low_ref):
        both = mm(coef[...], hi_ref[...])
        wide = both[:rows] + both[rows:] + mm(coef[:rows, :], low_ref[...])
        total = grad[...]
        for part in range(TABLE // width):
            s = block * (TABLE // width) + part
            tile = wide[:, part * width : (part + 1) * width]
            values[s] = tile
            for half in range(2):
                weights = in_ref[pl.ds((half * SCEN + s) * MSG1 + DUAL, 1), :]
                total = total + tile[:, half * LANES : (half + 1) * LANES] * weights
            for o in range(OPT):
                start = place_of(s, o) * MSG2
                for rank in range(MOST):
                    for half in range(2):
                        out_ref[
                            pl.ds(start + (rank * 2 + half) * 8, 8), :
                        ] = tile[
                            rank * LANES + o * 8 : rank * LANES + o * 8 + 8,
                            half * LANES : (half + 1) * LANES,
                        ]
        grad[...] = total

    tiles = out_ref.reshape(OUT_TILES)
    outs = []

    def send(*view):
        outs.append(
            pltpu.make_async_copy(tiles.at[view], out_hbm.at[view], out_sems.at[len(outs)])
        )
        outs[-1].start()

    def send_values(block):
        every, (z_lo, x_pair) = slice(None), divmod(block, 2)
        for first, last in ((0, 4), (5, 8), (9, 12), (13, 16)):
            send(every, z_lo, every, x_pair, slice(first, last))

    multiply(READY, hi_0, low_0)
    send_values(READY)
    for block in range(READY):
        for copy in copies[block]:
            copy.wait()
        multiply(block, hi_made.at[block], low_made.at[block])
        send_values(block)

    extra = in_ref[pl.ds(PAIR, DEVICES, stride=MSG1), :]
    bars = []
    for rank in range(MOST):
        cost, pos = extra[:, 2 * rank : 2 * rank + 1], extra[:, 2 * rank + 1 : 2 * rank + 2]
        gradient = jnp.sum(
            grad[rank * LANES : (rank + 1) * LANES, :], axis=1, keepdims=True
        )
        bars.append(2.0 * primal(pos, cost, gradient) - pos)
    bar = jnp.broadcast_to(jnp.concatenate(bars, axis=0), (rows, LANES))
    for s in range(SCEN):
        for half in range(2):
            pnl = values[s, :, half * LANES : (half + 1) * LANES] * bar
            pnl = jnp.broadcast_to(jnp.sum(pnl, axis=0, keepdims=True), (4, LANES))
            for o in (0, 1, 8, 9):
                first = place_of(s, o) * MSG2 + MSG2 - 2 + half
                out_ref[pl.ds(first, 4, stride=8 * MSG2), :] = pnl
    for tile in (4, 8, 12, 16):
        send(*[slice(None)] * 4, slice(tile, tile + 1))
    for out in outs:
        out.wait()


def tile_kernel(
    in_ref, choice_ref, dual_ref, base_ref, mass_ref, level_ref,
    tile_ref, pay_ref, dual_out, tile_hbm, sems,
):
    level = level_ref[0]
    level_bar = 2.0 * level_step(level, mass_ref[0]) - level
    weights = []
    for half in range(2):
        pnl = jnp.sum(
            in_ref[pl.ds(MSG2 - 2 + half, DEVICES, stride=MSG2), :], axis=0, keepdims=True
        )
        weights.append(
            dual(dual_ref[half : half + 1, :], base_ref[half : half + 1, :], pnl, level_bar)
        )
        dual_out[half : half + 1, :] = weights[half]
    new = jnp.concatenate(weights, axis=1)
    old = jnp.concatenate([dual_ref[0:1, :], dual_ref[1:2, :]], axis=1)
    tall = iota((8, 2 * LANES), 0)
    both = jnp.where(
        tall == 0,
        jnp.broadcast_to(old, (8, 2 * LANES)),
        jnp.where(tall == 1, jnp.broadcast_to(new, (8, 2 * LANES)), 0.0),
    )
    rows, copies = [], []
    for s in range(SCEN):
        arrived = jnp.concatenate(
            [
                jnp.concatenate(
                    [
                        in_ref[pl.ds((rank * 2 + half) * 8 + s, DEVICES, stride=MSG2), :]
                        for half in range(2)
                    ],
                    axis=1,
                )
                for rank in range(MOST)
            ],
            axis=0,
        )
        tile = pick(choice_ref[s], arrived)
        at = slice(s * LANES, (s + 1) * LANES)
        tile_ref[at, :] = tile
        if s < STORED:
            copies.append(pltpu.make_async_copy(tile_ref.at[at], tile_hbm.at[at], sems.at[s]))
            copies[s].start()
        rows.append(
            lax.dot_general(both, tile, NT, precision=HIGHEST, preferred_element_type=F32)
        )
    payload = jnp.concatenate(
        [r[0:1, :] for r in rows]
        + [r[1:2, :] for r in rows]
        + [weights[0] + weights[1], jnp.zeros((PAYLOAD - 17, LANES), F32)],
        axis=0,
    )
    for s in range(SCEN):
        pay_ref[s * PAYLOAD : (s + 1) * PAYLOAD, :] = payload
    for copy in copies:
        copy.wait()


def position_kernel(
    in_ref, tile_ref, cost_ref, pos_ref, kept_ref, mass_ref, level_ref,
    pos_out, pnl_out, bar_out, tile_hbm, level_out, sem,
):
    rest = slice(STORED * LANES, SCEN * LANES)
    keep = pltpu.make_async_copy(tile_ref.at[rest], tile_hbm.at[rest], sem)
    keep.start()
    total = in_ref[0:PAYLOAD, :]
    for s in range(1, SCEN):
        total = total + in_ref[s * PAYLOAD : (s + 1) * PAYLOAD, :]
    level = level_step(level_ref[0], mass_ref[0])
    later = level_step(level, jnp.sum(total[16:17, :]))
    level_out[0] = later
    bar_out[...] = jnp.full(bar_out.shape, 2.0 * later - level, F32)
    cost = cost_ref[...]
    first = primal(pos_ref[...], cost, total[0:8, :])
    second = primal(first, cost, total[8:16, :])
    pos_out[...] = second
    bar = 2.0 * second - first
    pnl = jnp.zeros((8, 2 * LANES), F32)
    odd = (iota((8, LANES), 0) & 1) == 1
    for s in range(SCEN):
        line = jnp.broadcast_to(bar[s : s + 1, :], (8, LANES))
        upper = line.astype(BF16).astype(F32)
        parts = jnp.where(odd, line - upper, upper).astype(BF16)
        hi, low = two(tile_ref[s * LANES : (s + 1) * LANES, :])
        pnl = pnl + mm(parts, hi) + mm(parts, low)
    pnl = pnl[0:1, :] + pnl[1:2, :]
    for o in range(OPT):
        for half in range(2):
            pnl_out[o * 2 + half : o * 2 + half + 1, :] = pnl[:, half * LANES : (half + 1) * LANES]
    keep.wait()


VMEM = pl.BlockSpec(memory_space=pltpu.VMEM)
HBM = pl.BlockSpec(memory_space=pltpu.HBM)
SMEM = pl.BlockSpec(memory_space=pltpu.SMEM)


def exchange(x, axes):
    return lax.all_to_all(x, axes, split_axis=0, concat_axis=0, tiled=True)


def shaped(*shape, dtype=F32):
    return jax.ShapeDtypeStruct(shape, dtype)


def value_scratch():
    return [
        pltpu.VMEM((DEVICES * MSG1, LANES), F32),
        pltpu.VMEM((BLOCKS - READY, BASE_ROWS, TABLE), F32),
        *[pltpu.VMEM((TERMS, TABLE), BF16)] * 2,
        *[pltpu.VMEM((READY, TERMS, TABLE), BF16)] * 2,
        pltpu.VMEM((2 * MOST * LANES, TERMS), BF16),
        pltpu.VMEM((SCEN, MOST * LANES, 2 * LANES), F32),
        pltpu.VMEM((MOST * LANES, LANES), F32),
        pltpu.VMEM((DEVICES * MSG2, LANES), F32),
        pltpu.SemaphoreType.DMA((4, READY)),
        pltpu.SemaphoreType.DMA((4 * BLOCKS + 4,)),
    ]


def on_device(
    option_coefs,
    underlying_of,
    log_return_mean,
    log_return_spread,
    cost,
    positions,
    base_loss,
    duals,
    threshold,
):
    own = underlying_of.reshape(SCEN, LANES)
    cost = cost.reshape(SCEN, LANES)
    positions = positions.reshape(SCEN, LANES)
    base_loss = base_loss.reshape(2, LANES)
    duals = duals.reshape(2, LANES)

    sent = pl.pallas_call(
        send_kernel,
        out_shape=shaped(DEVICES * MSG1, LANES),
        in_specs=[HBM] * 5,
        out_specs=HBM,
        scratch_shapes=[
            pltpu.VMEM((SCEN, LANES), jnp.int32),
            pltpu.VMEM((LANES, TERMS), F32),
            pltpu.VMEM((SCEN, LANES), F32),
            pltpu.VMEM((SCEN, LANES), F32),
            pltpu.VMEM((2, LANES), F32),
            pltpu.VMEM((DEVICES * MSG1, LANES), F32),
            pltpu.SemaphoreType.DMA((5,)),
            pltpu.SemaphoreType.DMA((PARTS,)),
        ],
        compiler_params=params(63),
    )(own, option_coefs, cost, positions, duals)
    got = exchange(sent.reshape(DEVICES, MSG1 // 2, 2, LANES), OPT_AXES + SCEN_AXES)
    got = got.reshape(DEVICES * MSG1, LANES)

    made = pl.BlockSpec((1, TERMS, TABLE), lambda i: (jnp.minimum(i, READY - 1), 0, 0))
    base, made_hi, made_low = pl.pallas_call(
        base_kernel,
        grid=(BLOCKS,),
        out_shape=[
            pltpu.HBM((BLOCKS, BASE_ROWS, TABLE), F32),
            *[pltpu.HBM((READY, TERMS, TABLE), BF16)] * 2,
        ],
        in_specs=[pl.BlockSpec((1, TABLE), lambda i: (0, i))] * 2,
        out_specs=[pl.BlockSpec((1, BASE_ROWS, TABLE), lambda i: (i, 0, 0)), made, made],
        compiler_params=params(12),
        cost_estimate=pl.CostEstimate(
            flops=2 * TERMS * SCENARIOS,
            bytes_accessed=TERMS * SCENARIOS,
            transcendentals=0,
        ),
    )(log_return_mean, log_return_spread)
    choice, mass = pl.pallas_call(
        choice_kernel,
        out_shape=[shaped(SCEN, LANES, MOST * LANES, dtype=BF16), shaped(1)],
        in_specs=[VMEM, HBM],
        out_specs=[VMEM, SMEM],
        scratch_shapes=[
            pltpu.VMEM((2 * SCEN * MSG1, LANES), F32),
            pltpu.SemaphoreType.DMA(()),
        ],
        compiler_params=params(4),
        cost_estimate=pl.CostEstimate(
            flops=TERMS * SCENARIOS, bytes_accessed=SCENARIOS, transcendentals=0
        ),
    )(own, got)

    values = pl.pallas_call(
        value_kernel,
        out_shape=shaped(*OUT_TILES),
        in_specs=[HBM] * 4,
        out_specs=HBM,
        scratch_shapes=value_scratch(),
        compiler_params=params(63),
    )(got, base, made_hi, made_low)
    arrived = exchange(values.reshape(DEVICES, MSG2 // 2, 2, LANES), PLACES)
    arrived = arrived.reshape(DEVICES * MSG2, LANES)

    tile, payload, first_duals, kept = pl.pallas_call(
        tile_kernel,
        out_shape=[
            shaped(SCEN * LANES, 2 * LANES),
            shaped(SCEN * PAYLOAD, LANES),
            shaped(2, LANES),
            shaped(SCEN * LANES, 2 * LANES),
        ],
        in_specs=[VMEM] * 4 + [SMEM] * 2,
        out_specs=[VMEM] * 3 + [HBM],
        scratch_shapes=[pltpu.SemaphoreType.DMA((STORED,))],
        compiler_params=params(12),
    )(arrived, choice, duals, base_loss, mass, threshold)
    gathered = exchange(payload.reshape(SCEN, PAYLOAD, LANES), SCEN_AXES[::-1])

    new_positions, part_pnl, level_bar, kept, level = pl.pallas_call(
        position_kernel,
        out_shape=[
            shaped(SCEN, LANES),
            shaped(OPT * 2, LANES),
            shaped(2, LANES),
            shaped(SCEN * LANES, 2 * LANES),
            shaped(1),
        ],
        in_specs=[VMEM] * 4 + [HBM] + [SMEM] * 2,
        out_specs=[VMEM] * 3 + [HBM, SMEM],
        input_output_aliases={4: 3},
        scratch_shapes=[pltpu.SemaphoreType.DMA(())],
        compiler_params=params(8),
    )(gathered.reshape(SCEN * PAYLOAD, LANES), tile, cost, positions, kept, mass, threshold)
    pnl = exchange(part_pnl.reshape(OPT, 2, LANES), OPT_AXES[::-1])

    new_duals = dual(first_duals, base_loss, jnp.sum(pnl, axis=0), level_bar)
    return (kept, new_positions.reshape(-1), new_duals.reshape(-1), level)


def solution(mesh):
    mesh = jax.sharding.Mesh(mesh.devices.reshape(SIZES), AXES)
    scen, opt = SCEN_AXES, OPT_AXES
    in_specs = (
        P(opt + scen, None),
        P(opt, None),
        P(AXES, None),
        P(AXES, None),
        P(opt),
        P(opt),
        P(scen),
        P(scen),
        P(),
    )
    out_specs = (P(opt, scen), P(opt), P(scen), P())
    return jax.shard_map(
        on_device, mesh=mesh, in_specs=in_specs, out_specs=out_specs, check_vma=False
    )
```

```python
import math

import jax
import jax.numpy as jnp
from jax import lax
from jax.experimental import pallas as pl
from jax.experimental.pallas import tpu as pltpu
from jax.sharding import PartitionSpec as P

LOW_END = -4.0
HIGH_END = 4.0
TAIL_LEVEL = 0.9
PRIMAL_STEP = 0.5
THRESH_STEP = 0.05
DUAL_STEP = 0.5

LANES = 128
SCEN = 8
OPT = 16
DEVICES = SCEN * OPT
TERMS = 1024
SCENARIOS = 2048
OPTIONS = 16384
MOST = 2
CHUNKS = TERMS // LANES
BASE = 32
TABLE = 512
BLOCKS = SCENARIOS // TABLE
READY = 3
BASE_ROWS = 4 * BASE + 8
PAIR = MOST * CHUNKS
DUAL = PAIR + 1
MSG1 = PAIR + 2
MSG2 = MOST * 16 + 2
PAYLOAD = 24
PARTS = 2
OUT_TILES = (2, 2, 4, 2, 17, 8, LANES)
STORED = 5
AXES = ("z_lo", "x", "z_hi", "y", "core")
SIZES = (2, 4, 2, 4, 2)
SCEN_AXES, OPT_AXES = AXES[:2], AXES[2:]
PLACES = ("z_hi", "z_lo", "y", "x", "core")
F32 = jnp.float32
BF16 = jnp.bfloat16
HIGHEST = lax.Precision.HIGHEST
NN = (((1,), (0,)), ((), ()))
NT = (((1,), (1,)), ((), ()))


def params(mib):
    return pltpu.CompilerParams(vmem_limit_bytes=int(mib * 1024 * 1024))


def iota(shape, axis):
    return lax.broadcasted_iota(jnp.int32, shape, axis)


def owner_of(place):
    return (place & (SCEN - 1)) * OPT + (place >> 3)


def place_of(scen, opt):
    (z_lo, x), (z_hi, rest) = divmod(scen, 4), divmod(opt, 8)
    y, core = divmod(rest, 2)
    return (((z_hi * 2 + z_lo) * 4 + y) * 4 + x) * 2 + core


def underlying_at(place):
    z_hi, z_lo, y, x = place >> 6, (place >> 5) & 1, (place >> 3) & 3, (place >> 1) & 3
    return (z_lo * 4 + x) * OPT + z_hi * 8 + y * 2 + (place & 1)


def mm(a, b, dims=NN):
    return lax.dot_general(a, b, dims, preferred_element_type=F32)


def three(x):
    hi = x.astype(BF16)
    rest = x - hi.astype(F32)
    mid = rest.astype(BF16)
    low = (rest - mid.astype(F32)).astype(BF16)
    return hi, mid, low


def two(x):
    hi = x.astype(BF16)
    return hi, (x - hi.astype(F32)).astype(BF16)


def pick(onehot, x, dims=NN):
    hi, mid, low = three(x)
    return mm(onehot, hi, dims) + mm(onehot, mid, dims) + mm(onehot, low, dims)


def level_step(level, mass):
    return level - THRESH_STEP * (1.0 - mass / ((1.0 - TAIL_LEVEL) * SCENARIOS))


def primal(position, cost, gradient):
    return jnp.clip(
        position - PRIMAL_STEP * (cost - gradient / math.sqrt(SCENARIOS)), -1.0, 1.0
    )


def dual(weights, base, pnl, level_bar):
    return jnp.clip(
        weights + DUAL_STEP * (base - pnl / math.sqrt(OPTIONS) - level_bar), 0.0, 1.0
    )


def send_kernel(
    own_hbm, coef_hbm, cost_hbm, pos_hbm, dual_hbm, out_hbm,
    own_ref, coef_ref, cost_ref, pos_ref, dual_ref, out_ref, sems, out_sems,
):
    pairs = (
        (own_hbm, own_ref),
        (cost_hbm, cost_ref),
        (pos_hbm, pos_ref),
        (dual_hbm, dual_ref),
        (coef_hbm, coef_ref),
    )
    copies = [pltpu.make_async_copy(a, b, sems.at[i]) for i, (a, b) in enumerate(pairs)]
    for copy in copies:
        copy.start()
    for copy in copies[:4]:
        copy.wait()
    row = lax.axis_index("z_lo") * 4 + lax.axis_index("x")
    half = lax.axis_index("core")
    square = (LANES, LANES)
    down, across = iota(square, 0), iota(square, 1)
    same = own_ref[pl.ds(row, 1), :] == owner_of(down)
    before = mm(
        same.astype(F32).astype(BF16), (down < across).astype(F32).astype(BF16)
    )
    cost = jnp.broadcast_to(cost_ref[pl.ds(row, 1), :], square)
    pos = jnp.broadcast_to(pos_ref[pl.ds(row, 1), :], square)
    chosen = [
        jnp.where(same & (before == float(rank)), 1.0, 0.0).astype(BF16)
        for rank in range(MOST)
    ]
    pair = jnp.zeros(square, F32)
    for rank in range(MOST):
        packed = jnp.where(
            down == 2 * rank, cost, jnp.where(down == 2 * rank + 1, pos, 0.0)
        )
        pair = pair + pick(chosen[rank], packed, NT)
    out_ref[pl.ds(PAIR, DEVICES, stride=MSG1), :] = pair
    out_ref[pl.ds(DUAL, DEVICES, stride=MSG1), :] = jnp.broadcast_to(
        dual_ref[pl.ds(half, 1), :], square
    )
    copies[4].wait()
    hi, mid = two(coef_ref[...])
    size = DEVICES // PARTS
    outs = []
    for part in range(PARTS):
        for rank in range(MOST):
            some = chosen[rank][part * size : (part + 1) * size, :]
            rows = mm(some, hi) + mm(some, mid)
            for chunk in range(CHUNKS):
                start = part * size * MSG1 + rank * CHUNKS + chunk
                out_ref[pl.ds(start, size, stride=MSG1), :] = rows[
                    :, chunk * LANES : (chunk + 1) * LANES
                ]
        at = slice(part * size * MSG1, (part + 1) * size * MSG1)
        outs.append(
            pltpu.make_async_copy(out_ref.at[at], out_hbm.at[at], out_sems.at[part])
        )
        outs[part].start()
    for out in outs:
        out.wait()


def turn(quarters, rest):
    x = rest * (2.0 * math.pi)
    z = x * x
    sin = x * (
        1.0 + z * (-1 / 6 + z * (1 / 120 + z * (-1 / 5040 + z * (1 / 362880))))
    )
    cos = 1.0 + z * (
        -1 / 2 + z * (1 / 24 + z * (-1 / 720 + z * (1 / 40320 - z * (1 / 3628800))))
    )
    swap = (quarters & 1) == 1
    cos_out = jnp.where(swap, sin, cos)
    sin_out = jnp.where(swap, cos, sin)
    cos_out = jnp.where(((quarters + 1) & 2) == 2, -cos_out, cos_out)
    sin_out = jnp.where((quarters & 2) == 2, -sin_out, sin_out)
    return cos_out, sin_out


def base_kernel(mean_ref, spread_ref, out_ref, hi_ref, low_ref):
    shape = (BASE, TABLE)
    mean = mean_ref[...]
    coarse = jnp.round(mean * 2048.0) * (1.0 / 2048.0)
    fine = mean - coarse
    step = iota(shape, 0)
    stepf = step.astype(F32)

    def base(scale, extra):
        turns = (stepf * scale) * coarse
        quarters = jnp.round(turns * 4.0)
        rest = (turns - quarters * 0.25) + (stepf * scale) * fine
        return turn(quarters.astype(jnp.int32) + extra, rest)

    cos_b, sin_b = base(1.0 / 16.0, step)
    cos_a, sin_a = base(BASE / 16.0, jnp.zeros_like(step))
    unit = math.pi / (HIGH_END - LOW_END)
    rate = spread_ref[...] * (-0.5 * unit * unit * math.log2(math.e))
    out_ref[0, 0:BASE, :] = cos_a * 0.25
    out_ref[0, BASE : 2 * BASE, :] = sin_a * 0.25
    out_ref[0, 2 * BASE : 3 * BASE, :] = cos_b
    out_ref[0, 3 * BASE : 4 * BASE, :] = sin_b
    out_ref[0, 4 * BASE :, :] = jnp.broadcast_to(rate, (8, TABLE))

    @pl.when(pl.program_id(0) < READY)
    def _():
        table(out_ref.at[0], hi_ref.at[0], low_ref.at[0])


def choice_kernel(own_ref, in_hbm, out_ref, mass_ref, in_ref, sem):
    first = pltpu.make_async_copy(in_hbm.at[0 : 2 * SCEN * MSG1], in_ref, sem)
    first.start()
    square = (LANES, LANES)
    down, across = iota(square, 0), iota(square, 1)
    names = jnp.concatenate(
        [own_ref[...].astype(F32), jnp.zeros((LANES - SCEN, LANES), F32)], axis=0
    ).T
    lower = (across < down).astype(F32).astype(BF16)
    owner = underlying_at(across).astype(F32)
    for s in range(SCEN):
        same = names[:, s : s + 1] == owner
        before = mm(lower, same.astype(F32).astype(BF16))
        for rank in range(MOST):
            out_ref[s, :, rank * LANES : (rank + 1) * LANES] = jnp.where(
                same & (before == float(rank)), 1.0, 0.0
            ).astype(BF16)
    first.wait()
    mass = jnp.zeros((1, LANES), F32)
    for place in range(2 * SCEN):
        at = place * MSG1 + DUAL
        mass = mass + in_ref[at : at + 1, :]
    mass_ref[0] = jnp.sum(mass)


def table(base_ref, hi_ref, low_ref):
    step = iota((BASE, LANES), 0)
    stepf = step.astype(F32)
    for half in range(TABLE // LANES):
        at = slice(half * LANES, (half + 1) * LANES)
        cos_b = base_ref[2 * BASE : 3 * BASE, at]
        sin_b = base_ref[3 * BASE : 4 * BASE, at]
        rate = base_ref[4 * BASE : 4 * BASE + 1, at]
        for a in range(BASE):
            k = stepf + float(BASE * a)
            value = (
                base_ref[a : a + 1, at] * cos_b
                - base_ref[BASE + a : BASE + a + 1, at] * sin_b
            ) * jnp.exp2((k * k) * rate)
            if a == 0:
                value = jnp.where(step == 0, value * 0.5, value)
            hi = value.astype(BF16)
            hi_ref[a * BASE : (a + 1) * BASE, at] = hi
            low_ref[a * BASE : (a + 1) * BASE, at] = (value - hi.astype(F32)).astype(BF16)


def value_kernel(
    in_hbm, base_hbm, hi_hbm, low_hbm, out_hbm,
    in_ref, base_ref, hi_0, low_0, hi_made, low_made, coef, values, grad, out_ref, sems, out_sems,
):
    width = 2 * LANES
    rows = MOST * LANES
    firsts = [
        pltpu.make_async_copy(base_hbm.at[READY], base_ref.at[0], sems.at[2, 0]),
        pltpu.make_async_copy(in_hbm, in_ref, sems.at[2, 1]),
    ]
    for copy in firsts:
        copy.start()
    copies = [
        (
            pltpu.make_async_copy(hi_hbm.at[block], hi_made.at[block], sems.at[0, block]),
            pltpu.make_async_copy(low_hbm.at[block], low_made.at[block], sems.at[1, block]),
        )
        for block in range(READY)
    ]
    for pair in copies:
        for copy in pair:
            copy.start()
    firsts[0].wait()
    table(base_ref.at[0], hi_0, low_0)
    firsts[1].wait()
    for rank in range(MOST):
        for chunk in range(CHUNKS):
            part = in_ref[pl.ds(rank * CHUNKS + chunk, DEVICES, stride=MSG1), :]
            hi = part.astype(BF16)
            at = slice(chunk * LANES, (chunk + 1) * LANES)
            coef[rank * LANES : (rank + 1) * LANES, at] = hi
            coef[rows + rank * LANES : rows + (rank + 1) * LANES, at] = (
                part - hi.astype(F32)
            ).astype(BF16)
    grad[...] = jnp.zeros_like(grad)

    def multiply(block, hi_ref, low_ref):
        both = mm(coef[...], hi_ref[...])
        wide = both[:rows] + both[rows:] + mm(coef[:rows, :], low_ref[...])
        total = grad[...]
        for part in range(TABLE // width):
            s = block * (TABLE // width) + part
            tile = wide[:, part * width : (part + 1) * width]
            values[s] = tile
            for half in range(2):
                weights = in_ref[pl.ds((half * SCEN + s) * MSG1 + DUAL, 1), :]
                total = total + tile[:, half * LANES : (half + 1) * LANES] * weights
            for o in range(OPT):
                start = place_of(s, o) * MSG2
                for rank in range(MOST):
                    for half in range(2):
                        out_ref[
                            pl.ds(start + (rank * 2 + half) * 8, 8), :
                        ] = tile[
                            rank * LANES + o * 8 : rank * LANES + o * 8 + 8,
                            half * LANES : (half + 1) * LANES,
                        ]
        grad[...] = total

    tiles = out_ref.reshape(OUT_TILES)
    outs = []

    def send(*view):
        outs.append(
            pltpu.make_async_copy(tiles.at[view], out_hbm.at[view], out_sems.at[len(outs)])
        )
        outs[-1].start()

    def send_values(block):
        every, (z_lo, x_pair) = slice(None), divmod(block, 2)
        for first, last in ((0, 4), (5, 8), (9, 12), (13, 16)):
            send(every, z_lo, every, x_pair, slice(first, last))

    multiply(READY, hi_0, low_0)
    send_values(READY)
    for block in range(READY):
        for copy in copies[block]:
            copy.wait()
        multiply(block, hi_made.at[block], low_made.at[block])
        send_values(block)

    extra = in_ref[pl.ds(PAIR, DEVICES, stride=MSG1), :]
    bars = []
    for rank in range(MOST):
        cost, pos = extra[:, 2 * rank : 2 * rank + 1], extra[:, 2 * rank + 1 : 2 * rank + 2]
        gradient = jnp.sum(
            grad[rank * LANES : (rank + 1) * LANES, :], axis=1, keepdims=True
        )
        bars.append(2.0 * primal(pos, cost, gradient) - pos)
    bar = jnp.broadcast_to(jnp.concatenate(bars, axis=0), (rows, LANES))
    for s in range(SCEN):
        for half in range(2):
            pnl = values[s, :, half * LANES : (half + 1) * LANES] * bar
            pnl = jnp.broadcast_to(jnp.sum(pnl, axis=0, keepdims=True), (4, LANES))
            for o in (0, 1, 8, 9):
                first = place_of(s, o) * MSG2 + MSG2 - 2 + half
                out_ref[pl.ds(first, 4, stride=8 * MSG2), :] = pnl
    for tile in (4, 8, 12, 16):
        send(*[slice(None)] * 4, slice(tile, tile + 1))
    for out in outs:
        out.wait()


def tile_kernel(
    in_ref, choice_ref, dual_ref, base_ref, mass_ref, level_ref,
    tile_ref, pay_ref, dual_out, tile_hbm, sems,
):
    level = level_ref[0]
    level_bar = 2.0 * level_step(level, mass_ref[0]) - level
    weights = []
    for half in range(2):
        pnl = jnp.sum(
            in_ref[pl.ds(MSG2 - 2 + half, DEVICES, stride=MSG2), :], axis=0, keepdims=True
        )
        weights.append(
            dual(dual_ref[half : half + 1, :], base_ref[half : half + 1, :], pnl, level_bar)
        )
        dual_out[half : half + 1, :] = weights[half]
    new = jnp.concatenate(weights, axis=1)
    old = jnp.concatenate([dual_ref[0:1, :], dual_ref[1:2, :]], axis=1)
    tall = iota((8, 2 * LANES), 0)
    both = jnp.where(
        tall == 0,
        jnp.broadcast_to(old, (8, 2 * LANES)),
        jnp.where(tall == 1, jnp.broadcast_to(new, (8, 2 * LANES)), 0.0),
    )
    rows, copies = [], []
    for s in range(SCEN):
        arrived = jnp.concatenate(
            [
                jnp.concatenate(
                    [
                        in_ref[pl.ds((rank * 2 + half) * 8 + s, DEVICES, stride=MSG2), :]
                        for half in range(2)
                    ],
                    axis=1,
                )
                for rank in range(MOST)
            ],
            axis=0,
        )
        tile = pick(choice_ref[s], arrived)
        at = slice(s * LANES, (s + 1) * LANES)
        tile_ref[at, :] = tile
        if s < STORED:
            copies.append(pltpu.make_async_copy(tile_ref.at[at], tile_hbm.at[at], sems.at[s]))
            copies[s].start()
        rows.append(
            lax.dot_general(both, tile, NT, precision=HIGHEST, preferred_element_type=F32)
        )
    payload = jnp.concatenate(
        [r[0:1, :] for r in rows]
        + [r[1:2, :] for r in rows]
        + [weights[0] + weights[1], jnp.zeros((PAYLOAD - 17, LANES), F32)],
        axis=0,
    )
    for s in range(SCEN):
        pay_ref[s * PAYLOAD : (s + 1) * PAYLOAD, :] = payload
    for copy in copies:
        copy.wait()


def position_kernel(
    in_ref, tile_ref, cost_ref, pos_ref, kept_ref, mass_ref, level_ref,
    pos_out, pnl_out, bar_out, tile_hbm, level_out, sem,
):
    rest = slice(STORED * LANES, SCEN * LANES)
    keep = pltpu.make_async_copy(tile_ref.at[rest], tile_hbm.at[rest], sem)
    keep.start()
    total = in_ref[0:PAYLOAD, :]
    for s in range(1, SCEN):
        total = total + in_ref[s * PAYLOAD : (s + 1) * PAYLOAD, :]
    level = level_step(level_ref[0], mass_ref[0])
    later = level_step(level, jnp.sum(total[16:17, :]))
    level_out[0] = later
    bar_out[...] = jnp.full(bar_out.shape, 2.0 * later - level, F32)
    cost = cost_ref[...]
    first = primal(pos_ref[...], cost, total[0:8, :])
    second = primal(first, cost, total[8:16, :])
    pos_out[...] = second
    bar = 2.0 * second - first
    pnl = jnp.zeros((8, 2 * LANES), F32)
    odd = (iota((8, LANES), 0) & 1) == 1
    for s in range(SCEN):
        line = jnp.broadcast_to(bar[s : s + 1, :], (8, LANES))
        upper = line.astype(BF16).astype(F32)
        parts = jnp.where(odd, line - upper, upper).astype(BF16)
        hi, low = two(tile_ref[s * LANES : (s + 1) * LANES, :])
        pnl = pnl + mm(parts, hi) + mm(parts, low)
    pnl = pnl[0:1, :] + pnl[1:2, :]
    for o in range(OPT):
        for half in range(2):
            pnl_out[o * 2 + half : o * 2 + half + 1, :] = pnl[:, half * LANES : (half + 1) * LANES]
    keep.wait()


VMEM = pl.BlockSpec(memory_space=pltpu.VMEM)
HBM = pl.BlockSpec(memory_space=pltpu.HBM)
SMEM = pl.BlockSpec(memory_space=pltpu.SMEM)


def exchange(x, axes):
    return lax.all_to_all(x, axes, split_axis=0, concat_axis=0, tiled=True)


def shaped(*shape, dtype=F32):
    return jax.ShapeDtypeStruct(shape, dtype)


def value_scratch():
    return [
        pltpu.VMEM((DEVICES * MSG1, LANES), F32),
        pltpu.VMEM((BLOCKS - READY, BASE_ROWS, TABLE), F32),
        *[pltpu.VMEM((TERMS, TABLE), BF16)] * 2,
        *[pltpu.VMEM((READY, TERMS, TABLE), BF16)] * 2,
        pltpu.VMEM((2 * MOST * LANES, TERMS), BF16),
        pltpu.VMEM((SCEN, MOST * LANES, 2 * LANES), F32),
        pltpu.VMEM((MOST * LANES, LANES), F32),
        pltpu.VMEM((DEVICES * MSG2, LANES), F32),
        pltpu.SemaphoreType.DMA((4, READY)),
        pltpu.SemaphoreType.DMA((4 * BLOCKS + 4,)),
    ]


def on_device(
    option_coefs,
    underlying_of,
    log_return_mean,
    log_return_spread,
    cost,
    positions,
    base_loss,
    duals,
    threshold,
):
    own = underlying_of.reshape(SCEN, LANES)
    cost = cost.reshape(SCEN, LANES)
    positions = positions.reshape(SCEN, LANES)
    base_loss = base_loss.reshape(2, LANES)
    duals = duals.reshape(2, LANES)

    sent = pl.pallas_call(
        send_kernel,
        out_shape=shaped(DEVICES * MSG1, LANES),
        in_specs=[HBM] * 5,
        out_specs=HBM,
        scratch_shapes=[
            pltpu.VMEM((SCEN, LANES), jnp.int32),
            pltpu.VMEM((LANES, TERMS), F32),
            pltpu.VMEM((SCEN, LANES), F32),
            pltpu.VMEM((SCEN, LANES), F32),
            pltpu.VMEM((2, LANES), F32),
            pltpu.VMEM((DEVICES * MSG1, LANES), F32),
            pltpu.SemaphoreType.DMA((5,)),
            pltpu.SemaphoreType.DMA((PARTS,)),
        ],
        compiler_params=params(63),
    )(own, option_coefs, cost, positions, duals)
    got = exchange(sent.reshape(DEVICES, MSG1 // 2, 2, LANES), OPT_AXES + SCEN_AXES)
    got = got.reshape(DEVICES * MSG1, LANES)

    made = pl.BlockSpec((1, TERMS, TABLE), lambda i: (jnp.minimum(i, READY - 1), 0, 0))
    base, made_hi, made_low = pl.pallas_call(
        base_kernel,
        grid=(BLOCKS,),
        out_shape=[
            pltpu.HBM((BLOCKS, BASE_ROWS, TABLE), F32),
            *[pltpu.HBM((READY, TERMS, TABLE), BF16)] * 2,
        ],
        in_specs=[pl.BlockSpec((1, TABLE), lambda i: (0, i))] * 2,
        out_specs=[pl.BlockSpec((1, BASE_ROWS, TABLE), lambda i: (i, 0, 0)), made, made],
        compiler_params=params(12),
        cost_estimate=pl.CostEstimate(
            flops=2 * TERMS * SCENARIOS,
            bytes_accessed=TERMS * SCENARIOS,
            transcendentals=0,
        ),
    )(log_return_mean, log_return_spread)
    choice, mass = pl.pallas_call(
        choice_kernel,
        out_shape=[shaped(SCEN, LANES, MOST * LANES, dtype=BF16), shaped(1)],
        in_specs=[VMEM, HBM],
        out_specs=[VMEM, SMEM],
        scratch_shapes=[
            pltpu.VMEM((2 * SCEN * MSG1, LANES), F32),
            pltpu.SemaphoreType.DMA(()),
        ],
        compiler_params=params(4),
        cost_estimate=pl.CostEstimate(
            flops=TERMS * SCENARIOS, bytes_accessed=SCENARIOS, transcendentals=0
        ),
    )(own, got)

    values = pl.pallas_call(
        value_kernel,
        out_shape=shaped(*OUT_TILES),
        in_specs=[HBM] * 4,
        out_specs=HBM,
        scratch_shapes=value_scratch(),
        compiler_params=params(63),
    )(got, base, made_hi, made_low)
    arrived = exchange(values.reshape(DEVICES, MSG2 // 2, 2, LANES), PLACES)
    arrived = arrived.reshape(DEVICES * MSG2, LANES)

    tile, payload, first_duals, kept = pl.pallas_call(
        tile_kernel,
        out_shape=[
            shaped(SCEN * LANES, 2 * LANES),
            shaped(SCEN * PAYLOAD, LANES),
            shaped(2, LANES),
            shaped(SCEN * LANES, 2 * LANES),
        ],
        in_specs=[VMEM] * 4 + [SMEM] * 2,
        out_specs=[VMEM] * 3 + [HBM],
        scratch_shapes=[pltpu.SemaphoreType.DMA((STORED,))],
        compiler_params=params(12),
    )(arrived, choice, duals, base_loss, mass, threshold)
    gathered = exchange(payload.reshape(SCEN, PAYLOAD, LANES), SCEN_AXES[::-1])

    new_positions, part_pnl, level_bar, kept, level = pl.pallas_call(
        position_kernel,
        out_shape=[
            shaped(SCEN, LANES),
            shaped(OPT * 2, LANES),
            shaped(2, LANES),
            shaped(SCEN * LANES, 2 * LANES),
            shaped(1),
        ],
        in_specs=[VMEM] * 4 + [HBM] + [SMEM] * 2,
        out_specs=[VMEM] * 3 + [HBM, SMEM],
        input_output_aliases={4: 3},
        scratch_shapes=[pltpu.SemaphoreType.DMA(())],
        compiler_params=params(8),
    )(gathered.reshape(SCEN * PAYLOAD, LANES), tile, cost, positions, kept, mass, threshold)
    pnl = exchange(part_pnl.reshape(OPT, 2, LANES), OPT_AXES[::-1])

    new_duals = dual(first_duals, base_loss, jnp.sum(pnl, axis=0), level_bar)
    return (kept, new_positions.reshape(-1), new_duals.reshape(-1), level)


def solution(mesh):
    mesh = jax.sharding.Mesh(mesh.devices.reshape(SIZES), AXES)
    scen, opt = SCEN_AXES, OPT_AXES
    in_specs = (
        P(opt + scen, None),
        P(opt, None),
        P(AXES, None),
        P(AXES, None),
        P(opt),
        P(opt),
        P(scen),
        P(scen),
        P(),
    )
    out_specs = (P(opt, scen), P(opt), P(scen), P())
    return jax.shard_map(
        on_device, mesh=mesh, in_specs=in_specs, out_specs=out_specs, check_vma=False
    )
```
